256 devices in a mesh: blk: 32 (over x_lo, z, core), tp: 8 (over x_hi, y).
Axes of the slice: x: 4 (x_hi: 2, x_lo: 2; x = x_hi * 2 + x_lo), y: 4, z: 8, core: 2. Of those that a mesh axis runs over, the one named last changes fastest.
Arguments:
- tokens: bfloat16 [8192, 8192], P('blk', 'tp'), may hold values from -6 to 6
- weight: bfloat16 [8192, 2048], P('tp'), may hold values from -0.0625 to 0.0625
- bank_a: bfloat16 [32, 8192, 32], P('blk', 'tp'), may hold values from -0.0625 to 0.0625
- bank_b: bfloat16 [32, 32, 1024], P('blk'), may hold values from -1.5 to 1.5
- tile_map: int32 [64, 1], P('blk'), may hold values from 0 to 31
- grad_out: bfloat16 [8192, 2048], P(('blk', 'tp')), may hold values from -6 to 6
Outputs:
- key_value_output: bfloat16 [8192, 2048], P(('blk', 'tp'))
- token_gradient: bfloat16 [8192, 8192], P('blk', 'tp')
- grad_a: float32 [32, 8192, 32], P('blk', 'tp')
- grad_b: float32 [32, 32, 1024], P('blk', None, 'tp')
The draws below stay inside these ranges and needn't reach their ends.
Inputs may be any that keep to these rules, and one draw needn't show every extreme that they name: `tile_map`: every one of the 32 adapters is the adapter of at least one tile.
All inputs are finite; a program needn't handle non-finite values.
Results may differ from the reference program's by a relative error of at most 0.003.
Values may be sent and summed in bfloat16 or wider, within the bound.
A program may use at most 64 MiB of HBM per device.

```python
import jax
import jax.numpy as jnp
from jax import lax

MODEL_WIDTH = 8192
KEY_VALUE_WIDTH = 1024
RANK = 16
TILE = 128
ADAPTERS = 32
TILES = 64
TOKENS = 8192


def steps_of(key, extent, pieces, smallest, top_value):
    loudness, own = 1.0, jax.random.fold_in(key, 6)
    for position, shards_of in pieces:
        steps = jnp.exp(jax.random.uniform(jax.random.fold_in(own, position), (shards_of,), jnp.float32, smallest / len(pieces), top_value / len(pieces)))
        loudness = loudness * jnp.repeat(steps, extent[position] // shards_of).reshape([-1 if axis == position else 1 for axis in range(len(extent))])
    return loudness


def distinct(own_key, rows, number_of, top, lift):
    ranking = jax.random.permutation(jax.random.fold_in(own_key, 1), number_of)
    pull = ranking
    for power in range(3):
        pull = pull * pull // number_of
    pull = pull * lift // number_of
    chance = jax.random.randint(jax.random.fold_in(own_key, 2), (rows, number_of), 0, 4096) + pull
    fixed_rows = jax.random.permutation(jax.random.fold_in(own_key, 3), rows)[jnp.arange(number_of) % rows]
    chance = jnp.where(jnp.arange(rows)[:, None] == fixed_rows[None, :], 1 << 14, chance)
    merit = chance * number_of + jnp.arange(number_of)
    return lax.top_k(merit.astype(jnp.int32), top)[1].astype(jnp.int32)


def normal_values(stream_key, shape, deviation, limit, split=(), kind=jnp.bfloat16):
    result = deviation * jax.random.normal(stream_key, shape, jnp.float32)
    if split:
        result = result * steps_of(stream_key, shape, split, -0.22, 0.18)
    return jnp.clip(result, -limit, limit).astype(kind)


def setup_inputs(seed: int = 0) -> dict:
    key_list = jax.random.split(jax.random.key(seed), 7)
    tokens = normal_values(key_list[0], (TOKENS, MODEL_WIDTH), 1.0, 6.0, ((0, 32), (1, 8)))
    weight = normal_values(key_list[1], (MODEL_WIDTH, 2 * KEY_VALUE_WIDTH), MODEL_WIDTH ** -0.5, 0.0625, ((0, 8),))
    bank_a = normal_values(key_list[2], (ADAPTERS, MODEL_WIDTH, 2 * RANK), MODEL_WIDTH ** -0.5, 0.0625, ((0, 32), (1, 8)))
    bank_b = normal_values(key_list[3], (ADAPTERS, 2 * RANK, KEY_VALUE_WIDTH), RANK ** -0.5, 1.5, ((0, 32),))
    tile_map = distinct(key_list[4], TILES, ADAPTERS, 1, 512)
    grad_out = normal_values(key_list[5], (TOKENS, 2 * KEY_VALUE_WIDTH), 1.0, 6.0, ((0, 256),))
    return {"tokens": tokens, "weight": weight, "bank_a": bank_a, "bank_b": bank_b, "tile_map": tile_map, "grad_out": grad_out}


adapter_scale = 0.5


def reference(tokens, weight, bank_a, bank_b, tile_map, grad_out):
    tile_index_list = tile_map[:, 0].astype(jnp.int32)
    overall_row_count = tokens.shape[0]
    tiles = overall_row_count // TILE
    token_tile_index = tokens.reshape(tiles, TILE, MODEL_WIDTH)
    gradient_per_tile = grad_out.reshape(tiles, TILE, 2 * KEY_VALUE_WIDTH)

    def single_tile(packed):
        token_rows, grad_rows, adapter = packed
        factor_down = bank_a[adapter]
        fac_b = bank_b[adapter]
        rank_act = jnp.dot(token_rows, factor_down, preferred_element_type=jnp.float32).astype(jnp.bfloat16)
        adapter_partial = jnp.concatenate([
            jnp.dot(rank_act[:, :RANK], fac_b[:RANK], preferred_element_type=jnp.float32),
            jnp.dot(rank_act[:, RANK:], fac_b[RANK:], preferred_element_type=jnp.float32)], axis=1)
        low_rank_gradient = jnp.concatenate([
            jnp.dot(grad_rows[:, :KEY_VALUE_WIDTH], fac_b[:RANK].T, preferred_element_type=jnp.float32),
            jnp.dot(grad_rows[:, KEY_VALUE_WIDTH:], fac_b[RANK:].T, preferred_element_type=jnp.float32)], axis=1).astype(jnp.bfloat16)
        backward_partial = jnp.dot(low_rank_gradient, factor_down.T, preferred_element_type=jnp.float32)
        tile_down_gradient = adapter_scale * jnp.dot(token_rows.T, low_rank_gradient, preferred_element_type=jnp.float32)
        tile_up_gradient = adapter_scale * jnp.concatenate([
            jnp.dot(rank_act[:, :RANK].T, grad_rows[:, :KEY_VALUE_WIDTH], preferred_element_type=jnp.float32),
            jnp.dot(rank_act[:, RANK:].T, grad_rows[:, KEY_VALUE_WIDTH:], preferred_element_type=jnp.float32)], axis=0)
        return adapter_partial, backward_partial, tile_down_gradient, tile_up_gradient

    adapter_partial, backward_partial, tile_down_gradient, tile_up_gradient = lax.map(single_tile, (token_tile_index, gradient_per_tile, tile_index_list))
    base_product = jnp.dot(tokens, weight, preferred_element_type=jnp.float32)
    key_value_output = (base_product + adapter_scale * adapter_partial.reshape(overall_row_count, 2 * KEY_VALUE_WIDTH)).astype(jnp.bfloat16)
    backward_pass = jnp.dot(grad_out, weight.T, preferred_element_type=jnp.float32)
    token_gradient = (backward_pass + adapter_scale * backward_partial.reshape(overall_row_count, MODEL_WIDTH)).astype(jnp.bfloat16)
    grad_a = jax.ops.segment_sum(tile_down_gradient, tile_index_list, num_segments=ADAPTERS)
    grad_b = jax.ops.segment_sum(tile_up_gradient, tile_index_list, num_segments=ADAPTERS)
    return key_value_output, token_gradient, grad_a, grad_b
```

```python
import jax
import jax.numpy as jnp
from jax import lax
from jax.sharding import PartitionSpec as P

adapter_scale = 0.5


def on_device(tokens, weight, bank_a, bank_b, tile_map, grad_out):
    f32, bf16 = jnp.float32, jnp.bfloat16
    tile_ids = tile_map[:, 0]
    rows, feats = tokens.shape
    tiles = tile_ids.shape[0]
    tile_rows = rows // tiles
    rank_two = bank_a.shape[2]
    rank_one = rank_two // 2
    kv_width = bank_b.shape[2]
    tp_count = lax.axis_size("tp")
    tp_id = lax.axis_index("tp")
    kv_dev = kv_width // tp_count
    col0 = tp_id * kv_dev

    b_cols = lax.dynamic_slice_in_dim(bank_b, col0, kv_dev, 2)
    all_b = lax.all_gather(b_cols, "blk", axis=0, tiled=True)
    all_a = lax.all_gather(bank_a, "blk", axis=0, tiled=True)
    grad_rows = lax.all_gather(grad_out, "tp", axis=0, tiled=True)

    fac_a = jnp.stack([all_a[tile_ids[t]] for t in range(tiles)])
    fac_b = jnp.stack([all_b[tile_ids[t]] for t in range(tiles)])

    tok_t = tokens.reshape(tiles, tile_rows, feats)
    g_t = grad_rows.reshape(tiles, tile_rows, 2 * kv_width)
    g_key = lax.dynamic_slice_in_dim(g_t, col0, kv_dev, 2)
    g_val = lax.dynamic_slice_in_dim(g_t, kv_width + col0, kv_dev, 2)

    act_part = jnp.einsum("tre,tek->trk", tok_t, fac_a, preferred_element_type=f32)
    grad_part = jnp.concatenate(
        [
            jnp.einsum("trc,tkc->trk", g_key, fac_b[:, :rank_one], preferred_element_type=f32),
            jnp.einsum("trc,tkc->trk", g_val, fac_b[:, rank_one:], preferred_element_type=f32),
        ],
        axis=2,
    )
    both = lax.psum(jnp.stack([act_part, grad_part]), "tp")
    rank_act = both[0].astype(bf16)
    rank_grad = both[1].astype(bf16)

    lora_key = jnp.einsum(
        "trk,tkc->trc", rank_act[:, :, :rank_one], fac_b[:, :rank_one], preferred_element_type=f32
    ).reshape(rows, kv_dev)
    lora_val = jnp.einsum(
        "trk,tkc->trc", rank_act[:, :, rank_one:], fac_b[:, rank_one:], preferred_element_type=f32
    ).reshape(rows, kv_dev)
    base = jnp.dot(tokens, weight, preferred_element_type=f32)
    base = lax.dynamic_update_slice_in_dim(
        base, lax.dynamic_slice_in_dim(base, col0, kv_dev, 1) + adapter_scale * lora_key, col0, 1
    )
    base = lax.dynamic_update_slice_in_dim(
        base,
        lax.dynamic_slice_in_dim(base, kv_width + col0, kv_dev, 1) + adapter_scale * lora_val,
        kv_width + col0,
        1,
    )
    key_value_output = lax.psum_scatter(base, "tp", scatter_dimension=0, tiled=True).astype(bf16)

    backward = jnp.dot(grad_rows, weight.T, preferred_element_type=f32)
    adapter_back = jnp.einsum("tru,tyu->try", rank_grad, fac_a, preferred_element_type=f32)
    token_gradient = (backward + adapter_scale * adapter_back.reshape(rows, feats)).astype(bf16)

    down_grad = adapter_scale * jnp.einsum("tre,trk->tek", tok_t, rank_grad, preferred_element_type=f32)
    up_grad = adapter_scale * jnp.concatenate(
        [
            jnp.einsum("trk,trc->tkc", rank_act[:, :, :rank_one], g_key, preferred_element_type=f32),
            jnp.einsum("trk,trc->tkc", rank_act[:, :, rank_one:], g_val, preferred_element_type=f32),
        ],
        axis=1,
    )
    size_a = feats * rank_two
    flat = jnp.concatenate([down_grad.reshape(tiles, -1), up_grad.reshape(tiles, -1)], axis=1)
    adapters = bank_a.shape[0] * lax.axis_size("blk")
    one_hot = (tile_ids[:, None] == jnp.arange(adapters, dtype=jnp.int32)[None, :]).astype(f32)
    dense = jnp.dot(one_hot.T, flat, precision=lax.Precision.HIGHEST, preferred_element_type=f32)
    summed = lax.psum_scatter(dense.reshape(adapters, -1, 128), "blk", scatter_dimension=0, tiled=True).reshape(bank_a.shape[0], -1)
    grad_a = summed[:, :size_a].reshape(bank_a.shape[0], feats, rank_two)
    grad_b = summed[:, size_a:].reshape(bank_a.shape[0], rank_two, kv_dev)
    return (key_value_output, token_gradient, grad_a, grad_b)


def solution(mesh):
    in_specs = (
        P("blk", "tp"),
        P("tp", None),
        P("blk", "tp", None),
        P("blk", None, None),
        P("blk", None),
        P(("blk", "tp"), None),
    )
    out_specs = (P(("blk", "tp"), None), P("blk", "tp"), P("blk", "tp", None), P("blk", None, "tp"))
    return jax.shard_map(
        on_device, mesh=mesh, in_specs=in_specs, out_specs=out_specs, check_vma=False
    )
```

```python
import functools

import jax
import jax.numpy as jnp
from jax import lax
from jax.experimental import pallas as pl
from jax.experimental.pallas import tpu as pltpu
from jax.sharding import PartitionSpec as P

adapter_scale = 0.5
MESH = pl.DeviceIdType.MESH


def _peer(axis, me, other, k, n):
    peer = lax.rem(me + k, n)
    return (other, peer) if axis == "tp" else (peer, other)


def _gather_kernel(axis, n, x_ref, o_ref, slots, send_sem, recv_sem):
    me = lax.axis_index(axis)
    other = lax.axis_index("blk" if axis == "tp" else "tp")
    barrier = pltpu.get_barrier_semaphore()
    for k in range(1, n):
        pl.semaphore_signal(
            barrier, inc=1, device_id=_peer(axis, me, other, k, n), device_id_type=MESH
        )
    pl.semaphore_wait(barrier, n - 1)
    sends = []
    for k in range(1, n):
        copy = pltpu.make_async_remote_copy(
            src_ref=x_ref,
            dst_ref=slots.at[me],
            send_sem=send_sem.at[k],
            recv_sem=recv_sem.at[me],
            device_id=_peer(axis, me, other, k, n),
            device_id_type=MESH,
        )
        copy.start()
        sends.append(copy)
    slots[me] = x_ref[...]
    for k in range(1, n):
        src = lax.rem(me + n - k, n)
        pltpu.make_async_remote_copy(
            src_ref=x_ref,
            dst_ref=slots.at[src],
            send_sem=send_sem.at[k],
            recv_sem=recv_sem.at[src],
            device_id=_peer(axis, me, other, n - k, n),
            device_id_type=MESH,
        ).wait_recv()
    for copy in sends:
        copy.wait_send()
    o_ref[...] = slots[...]


def gather_axis(x, axis, cid):
    n = lax.axis_size(axis)
    return pl.pallas_call(
        functools.partial(_gather_kernel, axis, n),
        out_shape=jax.ShapeDtypeStruct((n,) + x.shape, x.dtype),
        in_specs=[pl.BlockSpec(memory_space=pltpu.VMEM)],
        out_specs=pl.BlockSpec(memory_space=pltpu.VMEM),
        scratch_shapes=[
            pltpu.VMEM((n,) + x.shape, x.dtype),
            pltpu.SemaphoreType.DMA((n,)),
            pltpu.SemaphoreType.DMA((n,)),
        ],
        compiler_params=pltpu.CompilerParams(collective_id=cid, has_side_effects=True),
    )(x)


def on_device(tokens, weight, bank_a, bank_b, tile_map, grad_out):
    f32, bf16 = jnp.float32, jnp.bfloat16
    tile_ids = tile_map[:, 0]
    rows, feats = tokens.shape
    tiles = tile_ids.shape[0]
    tile_rows = rows // tiles
    rank_two = bank_a.shape[2]
    rank_one = rank_two // 2
    kv_width = bank_b.shape[2]
    tp_count = lax.axis_size("tp")
    tp_id = lax.axis_index("tp")
    kv_dev = kv_width // tp_count
    col0 = tp_id * kv_dev

    b_cols = lax.dynamic_slice_in_dim(bank_b, col0, kv_dev, 2)
    all_b = gather_axis(b_cols.reshape(-1, kv_dev), "blk", 0).reshape(-1, rank_two, kv_dev)
    all_a = lax.all_gather(bank_a, "blk", axis=0, tiled=True)
    grad_rows = gather_axis(grad_out, "tp", 1).reshape(rows, 2 * kv_width)

    fac_a = jnp.stack([all_a[tile_ids[t]] for t in range(tiles)])
    fac_b = jnp.stack([all_b[tile_ids[t]] for t in range(tiles)])

    tok_t = tokens.reshape(tiles, tile_rows, feats)
    g_t = grad_rows.reshape(tiles, tile_rows, 2 * kv_width)
    g_key = lax.dynamic_slice_in_dim(g_t, col0, kv_dev, 2)
    g_val = lax.dynamic_slice_in_dim(g_t, kv_width + col0, kv_dev, 2)

    act_part = jnp.einsum("tre,tek->trk", tok_t, fac_a, preferred_element_type=f32)
    grad_part = jnp.concatenate(
        [
            jnp.einsum("trc,tkc->trk", g_key, fac_b[:, :rank_one], preferred_element_type=f32),
            jnp.einsum("trc,tkc->trk", g_val, fac_b[:, rank_one:], preferred_element_type=f32),
        ],
        axis=2,
    )
    parts = jnp.stack([act_part, grad_part])
    both = gather_axis(parts.reshape(-1, 128), "tp", 2).sum(0).reshape(parts.shape)
    rank_act = both[0].astype(bf16)
    rank_grad = both[1].astype(bf16)

    lora_key = jnp.einsum(
        "trk,tkc->trc", rank_act[:, :, :rank_one], fac_b[:, :rank_one], preferred_element_type=f32
    ).reshape(rows, kv_dev)
    lora_val = jnp.einsum(
        "trk,tkc->trc", rank_act[:, :, rank_one:], fac_b[:, rank_one:], preferred_element_type=f32
    ).reshape(rows, kv_dev)
    base = jnp.dot(tokens, weight, preferred_element_type=f32)
    base = lax.dynamic_update_slice_in_dim(
        base, lax.dynamic_slice_in_dim(base, col0, kv_dev, 1) + adapter_scale * lora_key, col0, 1
    )
    base = lax.dynamic_update_slice_in_dim(
        base,
        lax.dynamic_slice_in_dim(base, kv_width + col0, kv_dev, 1) + adapter_scale * lora_val,
        kv_width + col0,
        1,
    )
    key_value_output = lax.psum_scatter(base, "tp", scatter_dimension=0, tiled=True).astype(bf16)

    backward = jnp.dot(grad_rows, weight.T, preferred_element_type=f32)
    adapter_back = jnp.einsum("tru,tyu->try", rank_grad, fac_a, preferred_element_type=f32)
    token_gradient = (backward + adapter_scale * adapter_back.reshape(rows, feats)).astype(bf16)

    down_grad = adapter_scale * jnp.einsum("tre,trk->tek", tok_t, rank_grad, preferred_element_type=f32)
    up_grad = adapter_scale * jnp.concatenate(
        [
            jnp.einsum("trk,trc->tkc", rank_act[:, :, :rank_one], g_key, preferred_element_type=f32),
            jnp.einsum("trk,trc->tkc", rank_act[:, :, rank_one:], g_val, preferred_element_type=f32),
        ],
        axis=1,
    )
    size_a = feats * rank_two
    flat = jnp.concatenate([down_grad.reshape(tiles, -1), up_grad.reshape(tiles, -1)], axis=1)
    adapters = bank_a.shape[0] * lax.axis_size("blk")
    one_hot = (tile_ids[:, None] == jnp.arange(adapters, dtype=jnp.int32)[None, :]).astype(f32)
    dense = jnp.dot(one_hot.T, flat, precision=lax.Precision.HIGHEST, preferred_element_type=f32)
    summed = lax.psum_scatter(dense.reshape(adapters, -1, 128), "blk", scatter_dimension=0, tiled=True).reshape(bank_a.shape[0], -1)
    grad_a = summed[:, :size_a].reshape(bank_a.shape[0], feats, rank_two)
    grad_b = summed[:, size_a:].reshape(bank_a.shape[0], rank_two, kv_dev)
    return (key_value_output, token_gradient, grad_a, grad_b)


def solution(mesh):
    in_specs = (
        P("blk", "tp"),
        P("tp", None),
        P("blk", "tp", None),
        P("blk", None, None),
        P("blk", None),
        P(("blk", "tp"), None),
    )
    out_specs = (P(("blk", "tp"), None), P("blk", "tp"), P("blk", "tp", None), P("blk", None, "tp"))
    return jax.shard_map(
        on_device, mesh=mesh, in_specs=in_specs, out_specs=out_specs, check_vma=False
    )
```

```python
import functools

import jax
import jax.numpy as jnp
from jax import lax
from jax.experimental import pallas as pl
from jax.experimental.pallas import tpu as pltpu
from jax.sharding import PartitionSpec as P

adapter_scale = 0.5
MESH = pl.DeviceIdType.MESH


def _peer(axis, me, other, k, n):
    peer = lax.rem(me + k, n)
    return (other, peer) if axis == "tp" else (peer, other)


def _gather_kernel(axis, n, x_ref, o_ref, slots, send_sem, recv_sem):
    me = lax.axis_index(axis)
    other = lax.axis_index("blk" if axis == "tp" else "tp")
    barrier = pltpu.get_barrier_semaphore()
    for k in range(1, n):
        pl.semaphore_signal(
            barrier, inc=1, device_id=_peer(axis, me, other, k, n), device_id_type=MESH
        )
    pl.semaphore_wait(barrier, n - 1)
    sends = []
    for k in range(1, n):
        copy = pltpu.make_async_remote_copy(
            src_ref=x_ref,
            dst_ref=slots.at[me],
            send_sem=send_sem.at[k],
            recv_sem=recv_sem.at[me],
            device_id=_peer(axis, me, other, k, n),
            device_id_type=MESH,
        )
        copy.start()
        sends.append(copy)
    slots[me] = x_ref[...]
    for k in range(1, n):
        src = lax.rem(me + n - k, n)
        pltpu.make_async_remote_copy(
            src_ref=x_ref,
            dst_ref=slots.at[src],
            send_sem=send_sem.at[k],
            recv_sem=recv_sem.at[src],
            device_id=_peer(axis, me, other, n - k, n),
            device_id_type=MESH,
        ).wait_recv()
    for copy in sends:
        copy.wait_send()
    o_ref[...] = slots[...]


def gather_axis(x, axis, cid):
    n = lax.axis_size(axis)
    return pl.pallas_call(
        functools.partial(_gather_kernel, axis, n),
        out_shape=jax.ShapeDtypeStruct((n,) + x.shape, x.dtype),
        in_specs=[pl.BlockSpec(memory_space=pltpu.VMEM)],
        out_specs=pl.BlockSpec(memory_space=pltpu.VMEM),
        scratch_shapes=[
            pltpu.VMEM((n,) + x.shape, x.dtype),
            pltpu.SemaphoreType.DMA((n,)),
            pltpu.SemaphoreType.DMA((n,)),
        ],
        compiler_params=pltpu.CompilerParams(collective_id=cid, has_side_effects=True),
    )(x)


def _swap(x, bit, count):
    return lax.ppermute(x, "blk", [(i, i ^ bit) for i in range(count)])


def reduce_to_owner(rows, ids, per):
    count = lax.axis_size("blk")
    me = lax.axis_index("blk")
    nbits = count.bit_length() - 1
    order = [count // 2] + [1 << k for k in range(nbits - 1)]
    sparse = min(2, nbits)
    for bit in order[:sparse]:
        rows = jnp.concatenate([rows, _swap(rows, bit, count)])
        ids = jnp.concatenate([ids, _swap(ids, bit, count)])
        owner = ids // per
        ids = jnp.where((ids >= 0) & ((owner & bit) == (me & bit)), ids, -1)
    rest = order[sparse:]
    owner = ids // per
    slot = ids % per
    for k, bit in enumerate(rest):
        slot = slot + ((owner & bit) != 0).astype(jnp.int32) * (per << (len(rest) - 1 - k))
    hit = (slot[:, None] == jnp.arange(per << len(rest))[None, :]) & (ids >= 0)[:, None]
    dense = jnp.sum(jnp.where(hit[:, :, None, None], rows[:, None], 0.0), axis=0)
    for bit in rest:
        half = dense.shape[0] // 2
        upper = (me & bit) != 0
        keep = jnp.where(upper, dense[half:], dense[:half])
        send = jnp.where(upper, dense[:half], dense[half:])
        dense = keep + _swap(send, bit, count)
    return dense


def on_device(tokens, weight, bank_a, bank_b, tile_map, grad_out):
    f32, bf16 = jnp.float32, jnp.bfloat16
    tile_ids = tile_map[:, 0]
    rows, feats = tokens.shape
    tiles = tile_ids.shape[0]
    tile_rows = rows // tiles
    rank_two = bank_a.shape[2]
    rank_one = rank_two // 2
    kv_width = bank_b.shape[2]
    tp_count = lax.axis_size("tp")
    tp_id = lax.axis_index("tp")
    kv_dev = kv_width // tp_count
    col0 = tp_id * kv_dev

    b_cols = lax.dynamic_slice_in_dim(bank_b, col0, kv_dev, 2)
    all_b = gather_axis(b_cols.reshape(-1, kv_dev), "blk", 0).reshape(-1, rank_two, kv_dev)
    all_a = lax.all_gather(bank_a, "blk", axis=0, tiled=True)
    grad_rows = gather_axis(grad_out, "tp", 1).reshape(rows, 2 * kv_width)

    fac_a = jnp.stack([all_a[tile_ids[t]] for t in range(tiles)])
    fac_b = jnp.stack([all_b[tile_ids[t]] for t in range(tiles)])

    tok_t = tokens.reshape(tiles, tile_rows, feats)
    g_t = grad_rows.reshape(tiles, tile_rows, 2 * kv_width)
    g_key = lax.dynamic_slice_in_dim(g_t, col0, kv_dev, 2)
    g_val = lax.dynamic_slice_in_dim(g_t, kv_width + col0, kv_dev, 2)

    act_part = jnp.einsum("tre,tek->trk", tok_t, fac_a, preferred_element_type=f32)
    grad_part = jnp.concatenate(
        [
            jnp.einsum("trc,tkc->trk", g_key, fac_b[:, :rank_one], preferred_element_type=f32),
            jnp.einsum("trc,tkc->trk", g_val, fac_b[:, rank_one:], preferred_element_type=f32),
        ],
        axis=2,
    )
    parts = jnp.stack([act_part, grad_part])
    both = gather_axis(parts.reshape(-1, 128), "tp", 2).sum(0).reshape(parts.shape)
    rank_act = both[0].astype(bf16)
    rank_grad = both[1].astype(bf16)

    lora_key = jnp.einsum(
        "trk,tkc->trc", rank_act[:, :, :rank_one], fac_b[:, :rank_one], preferred_element_type=f32
    ).reshape(rows, kv_dev)
    lora_val = jnp.einsum(
        "trk,tkc->trc", rank_act[:, :, rank_one:], fac_b[:, rank_one:], preferred_element_type=f32
    ).reshape(rows, kv_dev)
    base = jnp.dot(tokens, weight, preferred_element_type=f32)
    base = lax.dynamic_update_slice_in_dim(
        base, lax.dynamic_slice_in_dim(base, col0, kv_dev, 1) + adapter_scale * lora_key, col0, 1
    )
    base = lax.dynamic_update_slice_in_dim(
        base,
        lax.dynamic_slice_in_dim(base, kv_width + col0, kv_dev, 1) + adapter_scale * lora_val,
        kv_width + col0,
        1,
    )
    key_value_output = lax.psum_scatter(base, "tp", scatter_dimension=0, tiled=True).astype(bf16)

    backward = jnp.dot(grad_rows, weight.T, preferred_element_type=f32)
    adapter_back = jnp.einsum("tru,tyu->try", rank_grad, fac_a, preferred_element_type=f32)
    token_gradient = (backward + adapter_scale * adapter_back.reshape(rows, feats)).astype(bf16)

    down_grad = adapter_scale * jnp.einsum("tre,trk->tek", tok_t, rank_grad, preferred_element_type=f32)
    up_grad = adapter_scale * jnp.concatenate(
        [
            jnp.einsum("trk,trc->tkc", rank_act[:, :, :rank_one], g_key, preferred_element_type=f32),
            jnp.einsum("trk,trc->tkc", rank_act[:, :, rank_one:], g_val, preferred_element_type=f32),
        ],
        axis=1,
    )
    size_a = feats * rank_two
    flat = jnp.concatenate([down_grad.reshape(tiles, -1), up_grad.reshape(tiles, -1)], axis=1)
    summed = reduce_to_owner(flat.reshape(tiles, -1, 128), tile_ids, bank_a.shape[0]).reshape(bank_a.shape[0], -1)
    grad_a = summed[:, :size_a].reshape(bank_a.shape[0], feats, rank_two)
    grad_b = summed[:, size_a:].reshape(bank_a.shape[0], rank_two, kv_dev)
    return (key_value_output, token_gradient, grad_a, grad_b)


def solution(mesh):
    in_specs = (
        P("blk", "tp"),
        P("tp", None),
        P("blk", "tp", None),
        P("blk", None, None),
        P("blk", None),
        P(("blk", "tp"), None),
    )
    out_specs = (P(("blk", "tp"), None), P("blk", "tp"), P("blk", "tp", None), P("blk", None, "tp"))
    return jax.shard_map(
        on_device, mesh=mesh, in_specs=in_specs, out_specs=out_specs, check_vma=False
    )
```

```python
import functools

import jax
import jax.numpy as jnp
from jax import lax
from jax.experimental import pallas as pl
from jax.experimental.pallas import tpu as pltpu
from jax.sharding import PartitionSpec as P

adapter_scale = 0.5
MESH = pl.DeviceIdType.MESH


def _peer(axis, me, other, k, n):
    peer = lax.rem(me + k, n)
    return (other, peer) if axis == "tp" else (peer, other)


def _gather_kernel(axis, n, x_ref, o_ref, slots, send_sem, recv_sem):
    me = lax.axis_index(axis)
    other = lax.axis_index("blk" if axis == "tp" else "tp")
    barrier = pltpu.get_barrier_semaphore()
    for k in range(1, n):
        pl.semaphore_signal(
            barrier, inc=1, device_id=_peer(axis, me, other, k, n), device_id_type=MESH
        )
    pl.semaphore_wait(barrier, n - 1)
    sends = []
    for k in range(1, n):
        copy = pltpu.make_async_remote_copy(
            src_ref=x_ref,
            dst_ref=slots.at[me],
            send_sem=send_sem.at[k],
            recv_sem=recv_sem.at[me],
            device_id=_peer(axis, me, other, k, n),
            device_id_type=MESH,
        )
        copy.start()
        sends.append(copy)
    slots[me] = x_ref[...]
    for k in range(1, n):
        src = lax.rem(me + n - k, n)
        pltpu.make_async_remote_copy(
            src_ref=x_ref,
            dst_ref=slots.at[src],
            send_sem=send_sem.at[k],
            recv_sem=recv_sem.at[src],
            device_id=_peer(axis, me, other, n - k, n),
            device_id_type=MESH,
        ).wait_recv()
    for copy in sends:
        copy.wait_send()
    o_ref[...] = slots[...]


def gather_axis(x, axis, cid):
    n = lax.axis_size(axis)
    return pl.pallas_call(
        functools.partial(_gather_kernel, axis, n),
        out_shape=jax.ShapeDtypeStruct((n,) + x.shape, x.dtype),
        in_specs=[pl.BlockSpec(memory_space=pltpu.VMEM)],
        out_specs=pl.BlockSpec(memory_space=pltpu.VMEM),
        scratch_shapes=[
            pltpu.VMEM((n,) + x.shape, x.dtype),
            pltpu.SemaphoreType.DMA((n,)),
            pltpu.SemaphoreType.DMA((n,)),
        ],
        compiler_params=pltpu.CompilerParams(collective_id=cid, has_side_effects=True),
    )(x)


def _swap(x, bit, count):
    return lax.ppermute(x, "blk", [(i, i ^ bit) for i in range(count)])


def reduce_to_owner(rows, ids, per):
    count = lax.axis_size("blk")
    me = lax.axis_index("blk")
    nbits = count.bit_length() - 1
    order = [count // 2] + [1 << k for k in range(nbits - 1)]
    sparse = min(2, nbits)
    for bit in order[:sparse]:
        rows = jnp.concatenate([rows, _swap(rows, bit, count)])
        ids = jnp.concatenate([ids, _swap(ids, bit, count)])
        owner = ids // per
        ids = jnp.where((ids >= 0) & ((owner & bit) == (me & bit)), ids, -1)
    rest = order[sparse:]
    owner = ids // per
    slot = ids % per
    for k, bit in enumerate(rest):
        slot = slot + ((owner & bit) != 0).astype(jnp.int32) * (per << (len(rest) - 1 - k))
    hit = (slot[:, None] == jnp.arange(per << len(rest))[None, :]) & (ids >= 0)[:, None]
    dense = jnp.sum(jnp.where(hit[:, :, None, None], rows[:, None], 0.0), axis=0)
    for bit in rest:
        half = dense.shape[0] // 2
        upper = (me & bit) != 0
        keep = jnp.where(upper, dense[half:], dense[:half])
        send = jnp.where(upper, dense[:half], dense[half:])
        dense = keep + _swap(send, bit, count)
    return dense


def on_device(tokens, weight, bank_a, bank_b, tile_map, grad_out):
    f32, bf16 = jnp.float32, jnp.bfloat16
    tile_ids = tile_map[:, 0]
    rows, feats = tokens.shape
    tiles = tile_ids.shape[0]
    tile_rows = rows // tiles
    rank_two = bank_a.shape[2]
    rank_one = rank_two // 2
    kv_width = bank_b.shape[2]
    tp_count = lax.axis_size("tp")
    tp_id = lax.axis_index("tp")
    kv_dev = kv_width // tp_count
    col0 = tp_id * kv_dev

    b_cols = lax.dynamic_slice_in_dim(bank_b, col0, kv_dev, 2)
    local = bank_a.shape[0]
    a_len = feats * rank_two // 128
    packed = jnp.concatenate([bank_a.reshape(local, -1, 128), b_cols.reshape(local, -1, 128)], axis=1)
    all_ab = gather_axis(packed.reshape(-1, 128), "blk", 0).reshape(-1, packed.shape[1], 128)
    grad_rows = lax.all_gather(grad_out, "tp", axis=0, tiled=True)

    picked = jnp.stack([all_ab[tile_ids[t]] for t in range(tiles)])
    fac_a = picked[:, :a_len].reshape(tiles, feats, rank_two)
    fac_b = picked[:, a_len:].reshape(tiles, rank_two, kv_dev)

    tok_t = tokens.reshape(tiles, tile_rows, feats)
    act_part = jnp.einsum("tre,tek->trk", tok_t, fac_a, preferred_element_type=f32)
    rank_act = gather_axis(act_part.reshape(-1, 128), "tp", 2).sum(0).reshape(act_part.shape).astype(bf16)

    g_t = grad_rows.reshape(tiles, tile_rows, 2 * kv_width)
    g_key = lax.dynamic_slice_in_dim(g_t, col0, kv_dev, 2)
    g_val = lax.dynamic_slice_in_dim(g_t, kv_width + col0, kv_dev, 2)
    grad_part = jnp.concatenate(
        [
            jnp.einsum("trc,tkc->trk", g_key, fac_b[:, :rank_one], preferred_element_type=f32),
            jnp.einsum("trc,tkc->trk", g_val, fac_b[:, rank_one:], preferred_element_type=f32),
        ],
        axis=2,
    )
    rank_grad = gather_axis(grad_part.reshape(-1, 128), "tp", 3).sum(0).reshape(grad_part.shape).astype(bf16)

    lora_key = jnp.einsum(
        "trk,tkc->trc", rank_act[:, :, :rank_one], fac_b[:, :rank_one], preferred_element_type=f32
    ).reshape(rows, kv_dev)
    lora_val = jnp.einsum(
        "trk,tkc->trc", rank_act[:, :, rank_one:], fac_b[:, rank_one:], preferred_element_type=f32
    ).reshape(rows, kv_dev)
    base = jnp.dot(tokens, weight, preferred_element_type=f32)
    base = lax.dynamic_update_slice_in_dim(
        base, lax.dynamic_slice_in_dim(base, col0, kv_dev, 1) + adapter_scale * lora_key, col0, 1
    )
    base = lax.dynamic_update_slice_in_dim(
        base,
        lax.dynamic_slice_in_dim(base, kv_width + col0, kv_dev, 1) + adapter_scale * lora_val,
        kv_width + col0,
        1,
    )
    key_value_output = lax.psum_scatter(base, "tp", scatter_dimension=0, tiled=True).astype(bf16)

    backward = jnp.dot(grad_rows, weight.T, preferred_element_type=f32)
    adapter_back = jnp.einsum("tru,tyu->try", rank_grad, fac_a, preferred_element_type=f32)
    token_gradient = (backward + adapter_scale * adapter_back.reshape(rows, feats)).astype(bf16)

    down_grad = adapter_scale * jnp.einsum("tre,trk->tek", tok_t, rank_grad, preferred_element_type=f32)
    up_grad = adapter_scale * jnp.concatenate(
        [
            jnp.einsum("trk,trc->tkc", rank_act[:, :, :rank_one], g_key, preferred_element_type=f32),
            jnp.einsum("trk,trc->tkc", rank_act[:, :, rank_one:], g_val, preferred_element_type=f32),
        ],
        axis=1,
    )
    size_a = feats * rank_two
    flat = jnp.concatenate([down_grad.reshape(tiles, -1), up_grad.reshape(tiles, -1)], axis=1)
    summed = reduce_to_owner(flat.reshape(tiles, -1, 128), tile_ids, bank_a.shape[0]).reshape(bank_a.shape[0], -1)
    grad_a = summed[:, :size_a].reshape(bank_a.shape[0], feats, rank_two)
    grad_b = summed[:, size_a:].reshape(bank_a.shape[0], rank_two, kv_dev)
    return (key_value_output, token_gradient, grad_a, grad_b)


def solution(mesh):
    in_specs = (
        P("blk", "tp"),
        P("tp", None),
        P("blk", "tp", None),
        P("blk", None, None),
        P("blk", None),
        P(("blk", "tp"), None),
    )
    out_specs = (P(("blk", "tp"), None), P("blk", "tp"), P("blk", "tp", None), P("blk", None, "tp"))
    return jax.shard_map(
        on_device, mesh=mesh, in_specs=in_specs, out_specs=out_specs, check_vma=False
    )
```

```python
import functools

import jax
import jax.numpy as jnp
from jax import lax
from jax.experimental import pallas as pl
from jax.experimental.pallas import tpu as pltpu
from jax.sharding import PartitionSpec as P

adapter_scale = 0.5
MESH = pl.DeviceIdType.MESH


def _peer(axis, me, other, k, n):
    peer = lax.rem(me + k, n)
    return (other, peer) if axis == "tp" else (peer, other)


def _gather_kernel(axis, n, x_ref, o_ref, slots, send_sem, recv_sem):
    me = lax.axis_index(axis)
    other = lax.axis_index("blk" if axis == "tp" else "tp")
    barrier = pltpu.get_barrier_semaphore()
    for k in range(1, n):
        pl.semaphore_signal(
            barrier, inc=1, device_id=_peer(axis, me, other, k, n), device_id_type=MESH
        )
    pl.semaphore_wait(barrier, n - 1)
    sends = []
    for k in range(1, n):
        copy = pltpu.make_async_remote_copy(
            src_ref=x_ref,
            dst_ref=slots.at[me],
            send_sem=send_sem.at[k],
            recv_sem=recv_sem.at[me],
            device_id=_peer(axis, me, other, k, n),
            device_id_type=MESH,
        )
        copy.start()
        sends.append(copy)
    slots[me] = x_ref[...]
    for k in range(1, n):
        src = lax.rem(me + n - k, n)
        pltpu.make_async_remote_copy(
            src_ref=x_ref,
            dst_ref=slots.at[src],
            send_sem=send_sem.at[k],
            recv_sem=recv_sem.at[src],
            device_id=_peer(axis, me, other, n - k, n),
            device_id_type=MESH,
        ).wait_recv()
    for copy in sends:
        copy.wait_send()
    o_ref[...] = slots[...]


def gather_axis(x, axis, cid):
    n = lax.axis_size(axis)
    return pl.pallas_call(
        functools.partial(_gather_kernel, axis, n),
        out_shape=jax.ShapeDtypeStruct((n,) + x.shape, x.dtype),
        in_specs=[pl.BlockSpec(memory_space=pltpu.VMEM)],
        out_specs=pl.BlockSpec(memory_space=pltpu.VMEM),
        scratch_shapes=[
            pltpu.VMEM((n,) + x.shape, x.dtype),
            pltpu.SemaphoreType.DMA((n,)),
            pltpu.SemaphoreType.DMA((n,)),
        ],
        compiler_params=pltpu.CompilerParams(collective_id=cid, has_side_effects=True),
    )(x)


def _swap(x, bit, count):
    return lax.ppermute(x, "blk", [(i, i ^ bit) for i in range(count)])


def reduce_to_owner(rows, ids, per):
    count = lax.axis_size("blk")
    me = lax.axis_index("blk")
    nbits = count.bit_length() - 1
    order = [count // 2] + [1 << k for k in range(nbits - 1)]
    sparse = min(2, nbits)
    for bit in order[:sparse]:
        rows = jnp.concatenate([rows, _swap(rows, bit, count)])
        ids = jnp.concatenate([ids, _swap(ids, bit, count)])
        owner = ids // per
        ids = jnp.where((ids >= 0) & ((owner & bit) == (me & bit)), ids, -1)
    rest = order[sparse:]
    owner = ids // per
    slot = ids % per
    for k, bit in enumerate(rest):
        slot = slot + ((owner & bit) != 0).astype(jnp.int32) * (per << (len(rest) - 1 - k))
    hit = (slot[:, None] == jnp.arange(per << len(rest))[None, :]) & (ids >= 0)[:, None]
    dense = jnp.sum(jnp.where(hit[:, :, None, None], rows[:, None], 0.0), axis=0)
    for bit in rest:
        half = dense.shape[0] // 2
        upper = (me & bit) != 0
        keep = jnp.where(upper, dense[half:], dense[:half])
        send = jnp.where(upper, dense[:half], dense[half:])
        dense = keep + _swap(send, bit, count)
    return dense


def fetch_factors(rows, ids, per):
    count = lax.axis_size("blk")
    me = lax.axis_index("blk")
    nbits = count.bit_length() - 1
    order = [count // 2] + [1 << k for k in range(nbits - 1)]
    far, near = order[0], order[1]
    dense = order[2:][::-1]
    held = rows
    for bit in dense:
        got = _swap(held, bit, count)
        upper = (me & bit) != 0
        held = jnp.where(upper, jnp.concatenate([got, held]), jnp.concatenate([held, got]))
    group = far | near

    def lookup(want):
        owner = want // per
        k = want % per
        for i, bit in enumerate(dense):
            k = k + ((owner & bit) != 0).astype(jnp.int32) * (per << i)
        mine = (owner & group) == (me & group)
        found = jnp.take(held, k, axis=0)
        return mine, found, owner

    pair_ids = jnp.concatenate([ids, _swap(ids, far, count)])
    their_ids = _swap(pair_ids, near, count)
    mine, found, _ = lookup(their_ids)
    sent = jnp.where(mine[:, None, None], found, jnp.zeros_like(found))
    got = _swap(sent, near, count)
    mine, found, owner = lookup(pair_ids)
    side = (owner & far) == (me & far)
    cand = jnp.where(mine[:, None, None], found, got)
    half = ids.shape[0]
    got = _swap(cand[half:], far, count)
    return jnp.where(side[:half, None, None], cand[:half], got)


def on_device(tokens, weight, bank_a, bank_b, tile_map, grad_out):
    f32, bf16 = jnp.float32, jnp.bfloat16
    tile_ids = tile_map[:, 0]
    rows, feats = tokens.shape
    tiles = tile_ids.shape[0]
    tile_rows = rows // tiles
    rank_two = bank_a.shape[2]
    rank_one = rank_two // 2
    kv_width = bank_b.shape[2]
    tp_count = lax.axis_size("tp")
    tp_id = lax.axis_index("tp")
    kv_dev = kv_width // tp_count
    col0 = tp_id * kv_dev

    b_cols = lax.dynamic_slice_in_dim(bank_b, col0, kv_dev, 2)
    local = bank_a.shape[0]
    a_len = feats * rank_two // 128
    packed = jnp.concatenate([bank_a.reshape(local, -1, 128), b_cols.reshape(local, -1, 128)], axis=1)
    picked = fetch_factors(packed, tile_ids, local)
    grad_rows = lax.all_gather(grad_out, "tp", axis=0, tiled=True)

    fac_a = picked[:, :a_len].reshape(tiles, feats, rank_two)
    fac_b = picked[:, a_len:].reshape(tiles, rank_two, kv_dev)

    tok_t = tokens.reshape(tiles, tile_rows, feats)
    act_part = jnp.einsum("tre,tek->trk", tok_t, fac_a, preferred_element_type=f32)
    rank_act = gather_axis(act_part.reshape(-1, 128), "tp", 2).sum(0).reshape(act_part.shape).astype(bf16)

    g_t = grad_rows.reshape(tiles, tile_rows, 2 * kv_width)
    g_key = lax.dynamic_slice_in_dim(g_t, col0, kv_dev, 2)
    g_val = lax.dynamic_slice_in_dim(g_t, kv_width + col0, kv_dev, 2)
    grad_part = jnp.concatenate(
        [
            jnp.einsum("trc,tkc->trk", g_key, fac_b[:, :rank_one], preferred_element_type=f32),
            jnp.einsum("trc,tkc->trk", g_val, fac_b[:, rank_one:], preferred_element_type=f32),
        ],
        axis=2,
    )
    rank_grad = gather_axis(grad_part.reshape(-1, 128), "tp", 3).sum(0).reshape(grad_part.shape).astype(bf16)

    lora_key = jnp.einsum(
        "trk,tkc->trc", rank_act[:, :, :rank_one], fac_b[:, :rank_one], preferred_element_type=f32
    ).reshape(rows, kv_dev)
    lora_val = jnp.einsum(
        "trk,tkc->trc", rank_act[:, :, rank_one:], fac_b[:, rank_one:], preferred_element_type=f32
    ).reshape(rows, kv_dev)
    base = jnp.dot(tokens, weight, preferred_element_type=f32)
    base = lax.dynamic_update_slice_in_dim(
        base, lax.dynamic_slice_in_dim(base, col0, kv_dev, 1) + adapter_scale * lora_key, col0, 1
    )
    base = lax.dynamic_update_slice_in_dim(
        base,
        lax.dynamic_slice_in_dim(base, kv_width + col0, kv_dev, 1) + adapter_scale * lora_val,
        kv_width + col0,
        1,
    )
    key_value_output = lax.psum_scatter(base, "tp", scatter_dimension=0, tiled=True).astype(bf16)

    backward = jnp.dot(grad_rows, weight.T, preferred_element_type=f32)
    adapter_back = jnp.einsum("tru,tyu->try", rank_grad, fac_a, preferred_element_type=f32)
    token_gradient = (backward + adapter_scale * adapter_back.reshape(rows, feats)).astype(bf16)

    down_grad = adapter_scale * jnp.einsum("tre,trk->tek", tok_t, rank_grad, preferred_element_type=f32)
    up_grad = adapter_scale * jnp.concatenate(
        [
            jnp.einsum("trk,trc->tkc", rank_act[:, :, :rank_one], g_key, preferred_element_type=f32),
            jnp.einsum("trk,trc->tkc", rank_act[:, :, rank_one:], g_val, preferred_element_type=f32),
        ],
        axis=1,
    )
    size_a = feats * rank_two
    flat = jnp.concatenate([down_grad.reshape(tiles, -1), up_grad.reshape(tiles, -1)], axis=1)
    summed = reduce_to_owner(flat.reshape(tiles, -1, 128), tile_ids, bank_a.shape[0]).reshape(bank_a.shape[0], -1)
    grad_a = summed[:, :size_a].reshape(bank_a.shape[0], feats, rank_two)
    grad_b = summed[:, size_a:].reshape(bank_a.shape[0], rank_two, kv_dev)
    return (key_value_output, token_gradient, grad_a, grad_b)


def solution(mesh):
    in_specs = (
        P("blk", "tp"),
        P("tp", None),
        P("blk", "tp", None),
        P("blk", None, None),
        P("blk", None),
        P(("blk", "tp"), None),
    )
    out_specs = (P(("blk", "tp"), None), P("blk", "tp"), P("blk", "tp", None), P("blk", None, "tp"))
    return jax.shard_map(
        on_device, mesh=mesh, in_specs=in_specs, out_specs=out_specs, check_vma=False
    )
```

```python
import functools

import jax
import jax.numpy as jnp
from jax import lax
from jax.experimental import pallas as pl
from jax.experimental.pallas import tpu as pltpu
from jax.sharding import PartitionSpec as P

adapter_scale = 0.5
MESH = pl.DeviceIdType.MESH


def _peer(axis, me, other, k, n):
    peer = lax.rem(me + k, n)
    return (other, peer) if axis == "tp" else (peer, other)


def _gather_kernel(axis, n, x_ref, o_ref, slots, send_sem, recv_sem):
    me = lax.axis_index(axis)
    other = lax.axis_index("blk" if axis == "tp" else "tp")
    barrier = pltpu.get_barrier_semaphore()
    for k in range(1, n):
        pl.semaphore_signal(
            barrier, inc=1, device_id=_peer(axis, me, other, k, n), device_id_type=MESH
        )
    pl.semaphore_wait(barrier, n - 1)
    sends = []
    for k in range(1, n):
        copy = pltpu.make_async_remote_copy(
            src_ref=x_ref,
            dst_ref=slots.at[me],
            send_sem=send_sem.at[k],
            recv_sem=recv_sem.at[me],
            device_id=_peer(axis, me, other, k, n),
            device_id_type=MESH,
        )
        copy.start()
        sends.append(copy)
    slots[me] = x_ref[...]
    for k in range(1, n):
        src = lax.rem(me + n - k, n)
        pltpu.make_async_remote_copy(
            src_ref=x_ref,
            dst_ref=slots.at[src],
            send_sem=send_sem.at[k],
            recv_sem=recv_sem.at[src],
            device_id=_peer(axis, me, other, n - k, n),
            device_id_type=MESH,
        ).wait_recv()
    for copy in sends:
        copy.wait_send()
    o_ref[...] = slots[...]


def gather_axis(x, axis, cid):
    n = lax.axis_size(axis)
    return pl.pallas_call(
        functools.partial(_gather_kernel, axis, n),
        out_shape=jax.ShapeDtypeStruct((n,) + x.shape, x.dtype),
        in_specs=[pl.BlockSpec(memory_space=pltpu.VMEM)],
        out_specs=pl.BlockSpec(memory_space=pltpu.VMEM),
        scratch_shapes=[
            pltpu.VMEM((n,) + x.shape, x.dtype),
            pltpu.SemaphoreType.DMA((n,)),
            pltpu.SemaphoreType.DMA((n,)),
        ],
        compiler_params=pltpu.CompilerParams(collective_id=cid, has_side_effects=True),
    )(x)


def _swap(x, bit, count):
    return lax.ppermute(x, "blk", [(i, i ^ bit) for i in range(count)])


def reduce_to_owner(rows, ids, per):
    count = lax.axis_size("blk")
    me = lax.axis_index("blk")
    nbits = count.bit_length() - 1
    order = [count // 2] + [1 << k for k in range(nbits - 1)]
    sparse = min(2, nbits)
    for bit in order[:sparse]:
        rows = jnp.concatenate([rows, _swap(rows, bit, count)])
        ids = jnp.concatenate([ids, _swap(ids, bit, count)])
        owner = ids // per
        ids = jnp.where((ids >= 0) & ((owner & bit) == (me & bit)), ids, -1)
    rest = order[sparse:]
    owner = ids // per
    slot = ids % per
    for k, bit in enumerate(rest):
        slot = slot + ((owner & bit) != 0).astype(jnp.int32) * (per << (len(rest) - 1 - k))
    hit = (slot[:, None] == jnp.arange(per << len(rest))[None, :]) & (ids >= 0)[:, None]
    dense = jnp.sum(jnp.where(hit[:, :, None, None], rows[:, None], 0.0), axis=0)
    for bit in rest:
        half = dense.shape[0] // 2
        upper = (me & bit) != 0
        keep = jnp.where(upper, dense[half:], dense[:half])
        send = jnp.where(upper, dense[:half], dense[half:])
        dense = keep + _swap(send, bit, count)
    return dense


def gather_tp(x):
    count = lax.axis_size("tp")
    me = lax.axis_index("tp")
    held = x[None]
    bit = count // 2
    while bit:
        got = lax.ppermute(held, "tp", [(i, i ^ bit) for i in range(count)])
        upper = (me & bit) != 0
        held = jnp.where(upper, jnp.stack([got, held], axis=1), jnp.stack([held, got], axis=1))
        held = held.reshape((-1,) + x.shape)
        bit //= 2
    return held.reshape((-1,) + x.shape[1:])


def fetch_factors(rows, ids, per):
    count = lax.axis_size("blk")
    me = lax.axis_index("blk")
    nbits = count.bit_length() - 1
    order = [count // 2] + [1 << k for k in range(nbits - 1)]
    far, near = order[0], order[1]
    dense = order[2:][::-1]
    held = rows
    for bit in dense:
        got = _swap(held, bit, count)
        upper = (me & bit) != 0
        held = jnp.where(upper, jnp.concatenate([got, held]), jnp.concatenate([held, got]))
    group = far | near

    def lookup(want):
        owner = want // per
        k = want % per
        for i, bit in enumerate(dense):
            k = k + ((owner & bit) != 0).astype(jnp.int32) * (per << i)
        mine = (owner & group) == (me & group)
        found = jnp.take(held, k, axis=0)
        return mine, found, owner

    pair_ids = jnp.concatenate([ids, _swap(ids, far, count)])
    their_ids = _swap(pair_ids, near, count)
    mine, found, _ = lookup(their_ids)
    sent = jnp.where(mine[:, None, None], found, jnp.zeros_like(found))
    got = _swap(sent, near, count)
    mine, found, owner = lookup(pair_ids)
    side = (owner & far) == (me & far)
    cand = jnp.where(mine[:, None, None], found, got)
    half = ids.shape[0]
    got = _swap(cand[half:], far, count)
    return jnp.where(side[:half, None, None], cand[:half], got)


def on_device(tokens, weight, bank_a, bank_b, tile_map, grad_out):
    f32, bf16 = jnp.float32, jnp.bfloat16
    tile_ids = tile_map[:, 0]
    rows, feats = tokens.shape
    tiles = tile_ids.shape[0]
    tile_rows = rows // tiles
    rank_two = bank_a.shape[2]
    rank_one = rank_two // 2
    kv_width = bank_b.shape[2]
    tp_count = lax.axis_size("tp")
    tp_id = lax.axis_index("tp")
    kv_dev = kv_width // tp_count
    col0 = tp_id * kv_dev

    b_cols = lax.dynamic_slice_in_dim(bank_b, col0, kv_dev, 2)
    local = bank_a.shape[0]
    a_len = feats * rank_two // 128
    packed = jnp.concatenate([bank_a.reshape(local, -1, 128), b_cols.reshape(local, -1, 128)], axis=1)
    picked = fetch_factors(packed, tile_ids, local)
    grad_rows = gather_tp(grad_out)

    fac_a = picked[:, :a_len].reshape(tiles, feats, rank_two)
    fac_b = picked[:, a_len:].reshape(tiles, rank_two, kv_dev)

    tok_t = tokens.reshape(tiles, tile_rows, feats)
    act_part = jnp.einsum("tre,tek->trk", tok_t, fac_a, preferred_element_type=f32)
    rank_act = gather_axis(act_part.reshape(-1, 128), "tp", 2).sum(0).reshape(act_part.shape).astype(bf16)

    g_t = grad_rows.reshape(tiles, tile_rows, 2 * kv_width)
    g_key = lax.dynamic_slice_in_dim(g_t, col0, kv_dev, 2)
    g_val = lax.dynamic_slice_in_dim(g_t, kv_width + col0, kv_dev, 2)
    grad_part = jnp.concatenate(
        [
            jnp.einsum("trc,tkc->trk", g_key, fac_b[:, :rank_one], preferred_element_type=f32),
            jnp.einsum("trc,tkc->trk", g_val, fac_b[:, rank_one:], preferred_element_type=f32),
        ],
        axis=2,
    )
    rank_grad = gather_axis(grad_part.reshape(-1, 128), "tp", 3).sum(0).reshape(grad_part.shape).astype(bf16)

    lora_key = jnp.einsum(
        "trk,tkc->trc", rank_act[:, :, :rank_one], fac_b[:, :rank_one], preferred_element_type=f32
    ).reshape(rows, kv_dev)
    lora_val = jnp.einsum(
        "trk,tkc->trc", rank_act[:, :, rank_one:], fac_b[:, rank_one:], preferred_element_type=f32
    ).reshape(rows, kv_dev)
    base = jnp.dot(tokens, weight, preferred_element_type=f32)
    base = lax.dynamic_update_slice_in_dim(
        base, lax.dynamic_slice_in_dim(base, col0, kv_dev, 1) + adapter_scale * lora_key, col0, 1
    )
    base = lax.dynamic_update_slice_in_dim(
        base,
        lax.dynamic_slice_in_dim(base, kv_width + col0, kv_dev, 1) + adapter_scale * lora_val,
        kv_width + col0,
        1,
    )
    key_value_output = lax.psum_scatter(base, "tp", scatter_dimension=0, tiled=True).astype(bf16)

    backward = jnp.dot(grad_rows, weight.T, preferred_element_type=f32)
    adapter_back = jnp.einsum("tru,tyu->try", rank_grad, fac_a, preferred_element_type=f32)
    token_gradient = (backward + adapter_scale * adapter_back.reshape(rows, feats)).astype(bf16)

    down_grad = adapter_scale * jnp.einsum("tre,trk->tek", tok_t, rank_grad, preferred_element_type=f32)
    up_grad = adapter_scale * jnp.concatenate(
        [
            jnp.einsum("trk,trc->tkc", rank_act[:, :, :rank_one], g_key, preferred_element_type=f32),
            jnp.einsum("trk,trc->tkc", rank_act[:, :, rank_one:], g_val, preferred_element_type=f32),
        ],
        axis=1,
    )
    size_a = feats * rank_two
    flat = jnp.concatenate([down_grad.reshape(tiles, -1), up_grad.reshape(tiles, -1)], axis=1)
    summed = reduce_to_owner(flat.reshape(tiles, -1, 128), tile_ids, bank_a.shape[0]).reshape(bank_a.shape[0], -1)
    grad_a = summed[:, :size_a].reshape(bank_a.shape[0], feats, rank_two)
    grad_b = summed[:, size_a:].reshape(bank_a.shape[0], rank_two, kv_dev)
    return (key_value_output, token_gradient, grad_a, grad_b)


def solution(mesh):
    in_specs = (
        P("blk", "tp"),
        P("tp", None),
        P("blk", "tp", None),
        P("blk", None, None),
        P("blk", None),
        P(("blk", "tp"), None),
    )
    out_specs = (P(("blk", "tp"), None), P("blk", "tp"), P("blk", "tp", None), P("blk", None, "tp"))
    return jax.shard_map(
        on_device, mesh=mesh, in_specs=in_specs, out_specs=out_specs, check_vma=False
    )
```

```python
import functools

import jax
import jax.numpy as jnp
from jax import lax
from jax.experimental import pallas as pl
from jax.experimental.pallas import tpu as pltpu
from jax.sharding import PartitionSpec as P

adapter_scale = 0.5
MESH = pl.DeviceIdType.MESH


def _peer(axis, me, other, k, n):
    peer = lax.rem(me + k, n)
    return (other, peer) if axis == "tp" else (peer, other)


def _gather_kernel(axis, n, x_ref, o_ref, slots, send_sem, recv_sem):
    me = lax.axis_index(axis)
    other = lax.axis_index("blk" if axis == "tp" else "tp")
    barrier = pltpu.get_barrier_semaphore()
    for k in range(1, n):
        pl.semaphore_signal(
            barrier, inc=1, device_id=_peer(axis, me, other, k, n), device_id_type=MESH
        )
    pl.semaphore_wait(barrier, n - 1)
    sends = []
    for k in range(1, n):
        copy = pltpu.make_async_remote_copy(
            src_ref=x_ref,
            dst_ref=slots.at[me],
            send_sem=send_sem.at[k],
            recv_sem=recv_sem.at[me],
            device_id=_peer(axis, me, other, k, n),
            device_id_type=MESH,
        )
        copy.start()
        sends.append(copy)
    slots[me] = x_ref[...]
    for k in range(1, n):
        src = lax.rem(me + n - k, n)
        pltpu.make_async_remote_copy(
            src_ref=x_ref,
            dst_ref=slots.at[src],
            send_sem=send_sem.at[k],
            recv_sem=recv_sem.at[src],
            device_id=_peer(axis, me, other, n - k, n),
            device_id_type=MESH,
        ).wait_recv()
    for copy in sends:
        copy.wait_send()
    o_ref[...] = slots[...]


def gather_axis(x, axis, cid):
    n = lax.axis_size(axis)
    return pl.pallas_call(
        functools.partial(_gather_kernel, axis, n),
        out_shape=jax.ShapeDtypeStruct((n,) + x.shape, x.dtype),
        in_specs=[pl.BlockSpec(memory_space=pltpu.VMEM)],
        out_specs=pl.BlockSpec(memory_space=pltpu.VMEM),
        scratch_shapes=[
            pltpu.VMEM((n,) + x.shape, x.dtype),
            pltpu.SemaphoreType.DMA((n,)),
            pltpu.SemaphoreType.DMA((n,)),
        ],
        compiler_params=pltpu.CompilerParams(collective_id=cid, has_side_effects=True),
    )(x)


def _swap(x, bit, count):
    return lax.ppermute(x, "blk", [(i, i ^ bit) for i in range(count)])


def reduce_to_owner(rows, ids, per):
    count = lax.axis_size("blk")
    me = lax.axis_index("blk")
    nbits = count.bit_length() - 1
    order = [count // 2] + [1 << k for k in range(nbits - 1)]
    sparse = min(2, nbits)
    for bit in order[:sparse]:
        rows = jnp.concatenate([rows, _swap(rows, bit, count)])
        ids = jnp.concatenate([ids, _swap(ids, bit, count)])
        owner = ids // per
        ids = jnp.where((ids >= 0) & ((owner & bit) == (me & bit)), ids, -1)
    rest = order[sparse:]
    owner = ids // per
    slot = ids % per
    for k, bit in enumerate(rest):
        slot = slot + ((owner & bit) != 0).astype(jnp.int32) * (per << (len(rest) - 1 - k))
    hit = (slot[:, None] == jnp.arange(per << len(rest))[None, :]) & (ids >= 0)[:, None]
    dense = jnp.sum(jnp.where(hit[:, :, None, None], rows[:, None], 0.0), axis=0)
    for bit in rest:
        half = dense.shape[0] // 2
        upper = (me & bit) != 0
        keep = jnp.where(upper, dense[half:], dense[:half])
        send = jnp.where(upper, dense[:half], dense[half:])
        dense = keep + _swap(send, bit, count)
    return dense


def gather_tp(x):
    count = lax.axis_size("tp")
    me = lax.axis_index("tp")
    held = x[None]
    bit = count // 2
    while bit:
        got = lax.ppermute(held, "tp", [(i, i ^ bit) for i in range(count)])
        upper = (me & bit) != 0
        held = jnp.where(upper, jnp.stack([got, held], axis=1), jnp.stack([held, got], axis=1))
        held = held.reshape((-1,) + x.shape)
        bit //= 2
    return held.reshape((-1,) + x.shape[1:])


def fetch_factors(rows, ids, per):
    count = lax.axis_size("blk")
    me = lax.axis_index("blk")
    nbits = count.bit_length() - 1
    order = [count // 2] + [1 << k for k in range(nbits - 1)]
    far, near = order[0], order[1]
    dense = order[2:][::-1]
    held = rows
    for bit in dense:
        got = _swap(held, bit, count)
        upper = (me & bit) != 0
        held = jnp.where(upper, jnp.concatenate([got, held]), jnp.concatenate([held, got]))
    group = far | near

    def lookup(want):
        owner = want // per
        k = want % per
        for i, bit in enumerate(dense):
            k = k + ((owner & bit) != 0).astype(jnp.int32) * (per << i)
        mine = (owner & group) == (me & group)
        found = jnp.take(held, k, axis=0)
        return mine, found, owner

    pair_ids = jnp.concatenate([ids, _swap(ids, far, count)])
    their_ids = _swap(pair_ids, near, count)
    mine, found, _ = lookup(their_ids)
    sent = jnp.where(mine[:, None, None], found, jnp.zeros_like(found))
    got = _swap(sent, near, count)
    mine, found, owner = lookup(pair_ids)
    side = (owner & far) == (me & far)
    cand = jnp.where(mine[:, None, None], found, got)
    half = ids.shape[0]
    got = _swap(cand[half:], far, count)
    return jnp.where(side[:half, None, None], cand[:half], got)


def on_device(tokens, weight, bank_a, bank_b, tile_map, grad_out):
    f32, bf16 = jnp.float32, jnp.bfloat16
    tile_ids = tile_map[:, 0]
    rows, feats = tokens.shape
    tiles = tile_ids.shape[0]
    tile_rows = rows // tiles
    rank_two = bank_a.shape[2]
    rank_one = rank_two // 2
    kv_width = bank_b.shape[2]
    tp_count = lax.axis_size("tp")
    tp_id = lax.axis_index("tp")
    kv_dev = kv_width // tp_count
    col0 = tp_id * kv_dev

    b_cols = lax.dynamic_slice_in_dim(bank_b, col0, kv_dev, 2)
    local = bank_a.shape[0]
    a_len = feats * rank_two // 128
    packed = jnp.concatenate([bank_a.reshape(local, -1, 128), b_cols.reshape(local, -1, 128)], axis=1)
    picked = fetch_factors(packed, tile_ids, local)
    grad_rows = gather_tp(grad_out)

    fac_a = picked[:, :a_len].reshape(tiles, feats, rank_two)
    fac_b = picked[:, a_len:].reshape(tiles, rank_two, kv_dev)

    tok_t = tokens.reshape(tiles, tile_rows, feats)
    act_part = jnp.einsum("tre,tek->trk", tok_t, fac_a, preferred_element_type=f32)

    g_t = grad_rows.reshape(tiles, tile_rows, 2 * kv_width)
    g_key = lax.dynamic_slice_in_dim(g_t, col0, kv_dev, 2)
    g_val = lax.dynamic_slice_in_dim(g_t, kv_width + col0, kv_dev, 2)
    grad_part = jnp.concatenate(
        [
            jnp.einsum("trc,tkc->trk", g_key, fac_b[:, :rank_one], preferred_element_type=f32),
            jnp.einsum("trc,tkc->trk", g_val, fac_b[:, rank_one:], preferred_element_type=f32),
        ],
        axis=2,
    )
    parts = jnp.stack([act_part, grad_part])
    both = gather_axis(parts.reshape(-1, 128), "tp", 2).sum(0).reshape(parts.shape)
    rank_act = both[0].astype(bf16)
    rank_grad = both[1].astype(bf16)

    lora_key = jnp.einsum(
        "trk,tkc->trc", rank_act[:, :, :rank_one], fac_b[:, :rank_one], preferred_element_type=f32
    ).reshape(rows, kv_dev)
    lora_val = jnp.einsum(
        "trk,tkc->trc", rank_act[:, :, rank_one:], fac_b[:, rank_one:], preferred_element_type=f32
    ).reshape(rows, kv_dev)
    base = jnp.dot(tokens, weight, preferred_element_type=f32)
    base = lax.dynamic_update_slice_in_dim(
        base, lax.dynamic_slice_in_dim(base, col0, kv_dev, 1) + adapter_scale * lora_key, col0, 1
    )
    base = lax.dynamic_update_slice_in_dim(
        base,
        lax.dynamic_slice_in_dim(base, kv_width + col0, kv_dev, 1) + adapter_scale * lora_val,
        kv_width + col0,
        1,
    )
    key_value_output = lax.psum_scatter(base, "tp", scatter_dimension=0, tiled=True).astype(bf16)

    backward = jnp.dot(grad_rows, weight.T, preferred_element_type=f32)
    adapter_back = jnp.einsum("tru,tyu->try", rank_grad, fac_a, preferred_element_type=f32)
    token_gradient = (backward + adapter_scale * adapter_back.reshape(rows, feats)).astype(bf16)

    down_grad = adapter_scale * jnp.einsum("tre,trk->tek", tok_t, rank_grad, preferred_element_type=f32)
    up_grad = adapter_scale * jnp.concatenate(
        [
            jnp.einsum("trk,trc->tkc", rank_act[:, :, :rank_one], g_key, preferred_element_type=f32),
            jnp.einsum("trk,trc->tkc", rank_act[:, :, rank_one:], g_val, preferred_element_type=f32),
        ],
        axis=1,
    )
    size_a = feats * rank_two
    flat = jnp.concatenate([down_grad.reshape(tiles, -1), up_grad.reshape(tiles, -1)], axis=1)
    summed = reduce_to_owner(flat.reshape(tiles, -1, 128), tile_ids, bank_a.shape[0]).reshape(bank_a.shape[0], -1)
    grad_a = summed[:, :size_a].reshape(bank_a.shape[0], feats, rank_two)
    grad_b = summed[:, size_a:].reshape(bank_a.shape[0], rank_two, kv_dev)
    return (key_value_output, token_gradient, grad_a, grad_b)


def solution(mesh):
    in_specs = (
        P("blk", "tp"),
        P("tp", None),
        P("blk", "tp", None),
        P("blk", None, None),
        P("blk", None),
        P(("blk", "tp"), None),
    )
    out_specs = (P(("blk", "tp"), None), P("blk", "tp"), P("blk", "tp", None), P("blk", None, "tp"))
    return jax.shard_map(
        on_device, mesh=mesh, in_specs=in_specs, out_specs=out_specs, check_vma=False
    )
```

```python
import functools

import jax
import jax.numpy as jnp
from jax import lax
from jax.experimental import pallas as pl
from jax.experimental.pallas import tpu as pltpu
from jax.sharding import PartitionSpec as P

adapter_scale = 0.5
MESH = pl.DeviceIdType.MESH


def _peer(axis, me, other, k, n):
    peer = lax.rem(me + k, n)
    return (other, peer) if axis == "tp" else (peer, other)


def _gather_kernel(axis, n, x_ref, o_ref, slots, send_sem, recv_sem):
    me = lax.axis_index(axis)
    other = lax.axis_index("blk" if axis == "tp" else "tp")
    barrier = pltpu.get_barrier_semaphore()
    for k in range(1, n):
        pl.semaphore_signal(
            barrier, inc=1, device_id=_peer(axis, me, other, k, n), device_id_type=MESH
        )
    pl.semaphore_wait(barrier, n - 1)
    sends = []
    for k in range(1, n):
        copy = pltpu.make_async_remote_copy(
            src_ref=x_ref,
            dst_ref=slots.at[me],
            send_sem=send_sem.at[k],
            recv_sem=recv_sem.at[me],
            device_id=_peer(axis, me, other, k, n),
            device_id_type=MESH,
        )
        copy.start()
        sends.append(copy)
    slots[me] = x_ref[...]
    for k in range(1, n):
        src = lax.rem(me + n - k, n)
        pltpu.make_async_remote_copy(
            src_ref=x_ref,
            dst_ref=slots.at[src],
            send_sem=send_sem.at[k],
            recv_sem=recv_sem.at[src],
            device_id=_peer(axis, me, other, n - k, n),
            device_id_type=MESH,
        ).wait_recv()
    for copy in sends:
        copy.wait_send()
    o_ref[...] = slots[...]


def gather_axis(x, axis, cid):
    n = lax.axis_size(axis)
    return pl.pallas_call(
        functools.partial(_gather_kernel, axis, n),
        out_shape=jax.ShapeDtypeStruct((n,) + x.shape, x.dtype),
        in_specs=[pl.BlockSpec(memory_space=pltpu.VMEM)],
        out_specs=pl.BlockSpec(memory_space=pltpu.VMEM),
        scratch_shapes=[
            pltpu.VMEM((n,) + x.shape, x.dtype),
            pltpu.SemaphoreType.DMA((n,)),
            pltpu.SemaphoreType.DMA((n,)),
        ],
        compiler_params=pltpu.CompilerParams(collective_id=cid, has_side_effects=True),
    )(x)


def _swap(x, bit, count):
    return lax.ppermute(x, "blk", [(i, i ^ bit) for i in range(count)])


def reduce_to_owner(rows, ids, per):
    count = lax.axis_size("blk")
    me = lax.axis_index("blk")
    nbits = count.bit_length() - 1
    order = [count // 2] + [1 << k for k in range(nbits - 1)]
    sparse = min(2, nbits)
    for bit in order[:sparse]:
        rows = jnp.concatenate([rows, _swap(rows, bit, count)])
        ids = jnp.concatenate([ids, _swap(ids, bit, count)])
        owner = ids // per
        ids = jnp.where((ids >= 0) & ((owner & bit) == (me & bit)), ids, -1)
    rest = order[sparse:]
    owner = ids // per
    slot = ids % per
    for k, bit in enumerate(rest):
        slot = slot + ((owner & bit) != 0).astype(jnp.int32) * (per << (len(rest) - 1 - k))
    hit = (slot[:, None] == jnp.arange(per << len(rest))[None, :]) & (ids >= 0)[:, None]
    dense = jnp.sum(jnp.where(hit[:, :, None, None], rows[:, None], 0.0), axis=0)
    for bit in rest:
        half = dense.shape[0] // 2
        upper = (me & bit) != 0
        keep = jnp.where(upper, dense[half:], dense[:half])
        send = jnp.where(upper, dense[:half], dense[half:])
        dense = keep + _swap(send, bit, count)
    return dense


def gather_tp(x):
    count = lax.axis_size("tp")
    me = lax.axis_index("tp")
    held = x[None]
    bit = count // 2
    while bit:
        got = lax.ppermute(held, "tp", [(i, i ^ bit) for i in range(count)])
        upper = (me & bit) != 0
        held = jnp.where(upper, jnp.stack([got, held], axis=1), jnp.stack([held, got], axis=1))
        held = held.reshape((-1,) + x.shape)
        bit //= 2
    return held.reshape((-1,) + x.shape[1:])


def reduce_scatter_tp(x):
    count = lax.axis_size("tp")
    me = lax.axis_index("tp")
    nbits = count.bit_length() - 1
    held = x.reshape((2,) * nbits + (x.shape[0] // count,) + x.shape[1:])
    for k in range(nbits):
        bit = 1 << k
        axis = nbits - 1 - k
        low = lax.index_in_dim(held, 0, axis, keepdims=False)
        high = lax.index_in_dim(held, 1, axis, keepdims=False)
        upper = (me & bit) != 0
        keep = jnp.where(upper, high, low)
        send = jnp.where(upper, low, high)
        held = keep + lax.ppermute(send, "tp", [(i, i ^ bit) for i in range(count)])
    return held


def fetch_factors(rows, ids, per):
    count = lax.axis_size("blk")
    me = lax.axis_index("blk")
    nbits = count.bit_length() - 1
    order = [count // 2] + [1 << k for k in range(nbits - 1)]
    far, near = order[0], order[1]
    dense = order[2:][::-1]
    held = rows
    for bit in dense:
        got = _swap(held, bit, count)
        upper = (me & bit) != 0
        held = jnp.where(upper, jnp.concatenate([got, held]), jnp.concatenate([held, got]))
    group = far | near

    def lookup(want):
        owner = want // per
        k = want % per
        for i, bit in enumerate(dense):
            k = k + ((owner & bit) != 0).astype(jnp.int32) * (per << i)
        mine = (owner & group) == (me & group)
        found = jnp.take(held, k, axis=0)
        return mine, found, owner

    pair_ids = jnp.concatenate([ids, _swap(ids, far, count)])
    their_ids = _swap(pair_ids, near, count)
    mine, found, _ = lookup(their_ids)
    sent = jnp.where(mine[:, None, None], found, jnp.zeros_like(found))
    got = _swap(sent, near, count)
    mine, found, owner = lookup(pair_ids)
    side = (owner & far) == (me & far)
    cand = jnp.where(mine[:, None, None], found, got)
    half = ids.shape[0]
    got = _swap(cand[half:], far, count)
    return jnp.where(side[:half, None, None], cand[:half], got)


def on_device(tokens, weight, bank_a, bank_b, tile_map, grad_out):
    f32, bf16 = jnp.float32, jnp.bfloat16
    tile_ids = tile_map[:, 0]
    rows, feats = tokens.shape
    tiles = tile_ids.shape[0]
    tile_rows = rows // tiles
    rank_two = bank_a.shape[2]
    rank_one = rank_two // 2
    kv_width = bank_b.shape[2]
    tp_count = lax.axis_size("tp")
    tp_id = lax.axis_index("tp")
    kv_dev = kv_width // tp_count
    col0 = tp_id * kv_dev

    b_cols = lax.dynamic_slice_in_dim(bank_b, col0, kv_dev, 2)
    local = bank_a.shape[0]
    a_len = feats * rank_two // 128
    packed = jnp.concatenate([bank_a.reshape(local, -1, 128), b_cols.reshape(local, -1, 128)], axis=1)
    picked = fetch_factors(packed, tile_ids, local)
    grad_rows = gather_tp(grad_out)

    fac_a = picked[:, :a_len].reshape(tiles, feats, rank_two)
    fac_b = picked[:, a_len:].reshape(tiles, rank_two, kv_dev)

    tok_t = tokens.reshape(tiles, tile_rows, feats)
    act_part = jnp.einsum("tre,tek->trk", tok_t, fac_a, preferred_element_type=f32)

    g_t = grad_rows.reshape(tiles, tile_rows, 2 * kv_width)
    g_key = lax.dynamic_slice_in_dim(g_t, col0, kv_dev, 2)
    g_val = lax.dynamic_slice_in_dim(g_t, kv_width + col0, kv_dev, 2)
    grad_part = jnp.concatenate(
        [
            jnp.einsum("trc,tkc->trk", g_key, fac_b[:, :rank_one], preferred_element_type=f32),
            jnp.einsum("trc,tkc->trk", g_val, fac_b[:, rank_one:], preferred_element_type=f32),
        ],
        axis=2,
    )
    base_out = reduce_scatter_tp(jnp.dot(tokens, weight, preferred_element_type=f32))

    parts = jnp.stack([act_part, grad_part])
    flat_parts = parts.reshape(-1, 128)
    payload = jnp.concatenate([flat_parts, fac_b.astype(f32).reshape(-1, 128)])
    got = gather_axis(payload, "tp", 2)
    both = got[:, : flat_parts.shape[0]].sum(0).reshape(parts.shape)
    rank_act = both[0].astype(bf16)
    rank_grad = both[1].astype(bf16)
    full_b = got[:, flat_parts.shape[0] :].reshape(tp_count, tiles, rank_two, kv_dev)
    full_b = full_b.transpose(1, 2, 0, 3).reshape(tiles, rank_two, kv_width).astype(bf16)

    out_rows = rows // tp_count
    mine = max(1, out_rows // tile_rows)
    span = min(out_rows, tile_rows)
    first = tp_id * out_rows
    my_act = lax.dynamic_slice(rank_act, (first // tile_rows, first % tile_rows, 0), (mine, span, rank_two))
    my_b = lax.dynamic_slice(full_b, (first // tile_rows, 0, 0), (mine, rank_two, kv_width))
    lora = jnp.concatenate(
        [
            jnp.einsum("trk,tkc->trc", my_act[:, :, :rank_one], my_b[:, :rank_one], preferred_element_type=f32),
            jnp.einsum("trk,tkc->trc", my_act[:, :, rank_one:], my_b[:, rank_one:], preferred_element_type=f32),
        ],
        axis=2,
    ).reshape(out_rows, 2 * kv_width)
    key_value_output = (base_out + adapter_scale * lora).astype(bf16)

    backward = jnp.dot(grad_rows, weight.T, preferred_element_type=f32)
    adapter_back = jnp.einsum("tru,tyu->try", rank_grad, fac_a, preferred_element_type=f32)
    token_gradient = (backward + adapter_scale * adapter_back.reshape(rows, feats)).astype(bf16)

    down_grad = adapter_scale * jnp.einsum("tre,trk->tek", tok_t, rank_grad, preferred_element_type=f32)
    up_grad = adapter_scale * jnp.concatenate(
        [
            jnp.einsum("trk,trc->tkc", rank_act[:, :, :rank_one], g_key, preferred_element_type=f32),
            jnp.einsum("trk,trc->tkc", rank_act[:, :, rank_one:], g_val, preferred_element_type=f32),
        ],
        axis=1,
    )
    size_a = feats * rank_two
    flat = jnp.concatenate([down_grad.reshape(tiles, -1), up_grad.reshape(tiles, -1)], axis=1)
    summed = reduce_to_owner(flat.reshape(tiles, -1, 128), tile_ids, bank_a.shape[0]).reshape(bank_a.shape[0], -1)
    grad_a = summed[:, :size_a].reshape(bank_a.shape[0], feats, rank_two)
    grad_b = summed[:, size_a:].reshape(bank_a.shape[0], rank_two, kv_dev)
    return (key_value_output, token_gradient, grad_a, grad_b)


def solution(mesh):
    in_specs = (
        P("blk", "tp"),
        P("tp", None),
        P("blk", "tp", None),
        P("blk", None, None),
        P("blk", None),
        P(("blk", "tp"), None),
    )
    out_specs = (P(("blk", "tp"), None), P("blk", "tp"), P("blk", "tp", None), P("blk", None, "tp"))
    return jax.shard_map(
        on_device, mesh=mesh, in_specs=in_specs, out_specs=out_specs, check_vma=False
    )
```

```python
import functools

import jax
import jax.numpy as jnp
from jax import lax
from jax.experimental import pallas as pl
from jax.experimental.pallas import tpu as pltpu
from jax.sharding import PartitionSpec as P

adapter_scale = 0.5
MESH = pl.DeviceIdType.MESH


def _peer(axis, me, other, k, n):
    peer = lax.rem(me + k, n)
    return (other, peer) if axis == "tp" else (peer, other)


def _gather_kernel(axis, n, x_ref, o_ref, slots, send_sem, recv_sem):
    me = lax.axis_index(axis)
    other = lax.axis_index("blk" if axis == "tp" else "tp")
    barrier = pltpu.get_barrier_semaphore()
    for k in range(1, n):
        pl.semaphore_signal(
            barrier, inc=1, device_id=_peer(axis, me, other, k, n), device_id_type=MESH
        )
    pl.semaphore_wait(barrier, n - 1)
    sends = []
    for k in range(1, n):
        copy = pltpu.make_async_remote_copy(
            src_ref=x_ref,
            dst_ref=slots.at[me],
            send_sem=send_sem.at[k],
            recv_sem=recv_sem.at[me],
            device_id=_peer(axis, me, other, k, n),
            device_id_type=MESH,
        )
        copy.start()
        sends.append(copy)
    slots[me] = x_ref[...]
    for k in range(1, n):
        src = lax.rem(me + n - k, n)
        pltpu.make_async_remote_copy(
            src_ref=x_ref,
            dst_ref=slots.at[src],
            send_sem=send_sem.at[k],
            recv_sem=recv_sem.at[src],
            device_id=_peer(axis, me, other, n - k, n),
            device_id_type=MESH,
        ).wait_recv()
    for copy in sends:
        copy.wait_send()
    o_ref[...] = slots[...]


def gather_axis(x, axis, cid):
    n = lax.axis_size(axis)
    return pl.pallas_call(
        functools.partial(_gather_kernel, axis, n),
        out_shape=jax.ShapeDtypeStruct((n,) + x.shape, x.dtype),
        in_specs=[pl.BlockSpec(memory_space=pltpu.VMEM)],
        out_specs=pl.BlockSpec(memory_space=pltpu.VMEM),
        scratch_shapes=[
            pltpu.VMEM((n,) + x.shape, x.dtype),
            pltpu.SemaphoreType.DMA((n,)),
            pltpu.SemaphoreType.DMA((n,)),
        ],
        compiler_params=pltpu.CompilerParams(collective_id=cid, has_side_effects=True),
    )(x)


def _swap(x, bit, count):
    return lax.ppermute(x, "blk", [(i, i ^ bit) for i in range(count)])


def reduce_to_owner(rows, ids, per):
    count = lax.axis_size("blk")
    me = lax.axis_index("blk")
    nbits = count.bit_length() - 1
    order = [count // 2] + [1 << k for k in range(nbits - 1)]
    sparse = min(2, nbits)
    for bit in order[:sparse]:
        rows = jnp.concatenate([rows, _swap(rows, bit, count)])
        ids = jnp.concatenate([ids, _swap(ids, bit, count)])
        owner = ids // per
        ids = jnp.where((ids >= 0) & ((owner & bit) == (me & bit)), ids, -1)
    rest = order[sparse:]
    owner = ids // per
    slot = ids % per
    for k, bit in enumerate(rest):
        slot = slot + ((owner & bit) != 0).astype(jnp.int32) * (per << (len(rest) - 1 - k))
    hit = (slot[:, None] == jnp.arange(per << len(rest))[None, :]) & (ids >= 0)[:, None]
    dense = jnp.sum(jnp.where(hit[:, :, None, None], rows[:, None], 0.0), axis=0)
    for bit in rest:
        half = dense.shape[0] // 2
        upper = (me & bit) != 0
        keep = jnp.where(upper, dense[half:], dense[:half])
        send = jnp.where(upper, dense[:half], dense[half:])
        dense = keep + _swap(send, bit, count)
    return dense


def gather_tp(x):
    count = lax.axis_size("tp")
    me = lax.axis_index("tp")
    held = x[None]
    bit = count // 2
    while bit:
        got = lax.ppermute(held, "tp", [(i, i ^ bit) for i in range(count)])
        upper = (me & bit) != 0
        held = jnp.where(upper, jnp.stack([got, held], axis=1), jnp.stack([held, got], axis=1))
        held = held.reshape((-1,) + x.shape)
        bit //= 2
    return held.reshape((-1,) + x.shape[1:])


def reduce_scatter_tp(x):
    count = lax.axis_size("tp")
    me = lax.axis_index("tp")
    nbits = count.bit_length() - 1
    held = x.reshape((2,) * nbits + (x.shape[0] // count,) + x.shape[1:])
    for k in range(nbits):
        bit = 1 << k
        axis = nbits - 1 - k
        low = lax.index_in_dim(held, 0, axis, keepdims=False)
        high = lax.index_in_dim(held, 1, axis, keepdims=False)
        upper = (me & bit) != 0
        keep = jnp.where(upper, high, low)
        send = jnp.where(upper, low, high)
        held = keep + lax.ppermute(send, "tp", [(i, i ^ bit) for i in range(count)])
    return held


def fetch_factors(rows, ids, per):
    count = lax.axis_size("blk")
    me = lax.axis_index("blk")
    nbits = count.bit_length() - 1
    order = [count // 2] + [1 << k for k in range(nbits - 1)]
    far, near = order[0], order[1]
    dense = order[2:][::-1]
    held = rows
    for bit in dense:
        got = _swap(held, bit, count)
        upper = (me & bit) != 0
        held = jnp.where(upper, jnp.concatenate([got, held]), jnp.concatenate([held, got]))
    group = far | near

    def lookup(want):
        owner = want // per
        k = want % per
        for i, bit in enumerate(dense):
            k = k + ((owner & bit) != 0).astype(jnp.int32) * (per << i)
        mine = (owner & group) == (me & group)
        found = jnp.take(held, k, axis=0)
        return mine, found, owner

    pair_ids = jnp.concatenate([ids, _swap(ids, far, count)])
    their_ids = _swap(pair_ids, near, count)
    mine, found, _ = lookup(their_ids)
    sent = jnp.where(mine[:, None, None], found, jnp.zeros_like(found))
    got = _swap(sent, near, count)
    mine, found, owner = lookup(pair_ids)
    side = (owner & far) == (me & far)
    cand = jnp.where(mine[:, None, None], found, got)
    half = ids.shape[0]
    got = _swap(cand[half:], far, count)
    return jnp.where(side[:half, None, None], cand[:half], got)


def on_device(tokens, weight, bank_a, bank_b, tile_map, grad_out):
    f32, bf16 = jnp.float32, jnp.bfloat16
    tile_ids = tile_map[:, 0]
    rows, feats = tokens.shape
    tiles = tile_ids.shape[0]
    tile_rows = rows // tiles
    rank_two = bank_a.shape[2]
    rank_one = rank_two // 2
    kv_width = bank_b.shape[2]
    tp_count = lax.axis_size("tp")
    tp_id = lax.axis_index("tp")
    kv_dev = kv_width // tp_count
    col0 = tp_id * kv_dev

    b_cols = lax.dynamic_slice_in_dim(bank_b, col0, kv_dev, 2)
    local = bank_a.shape[0]
    a_len = feats * rank_two // 128
    packed = jnp.concatenate([bank_a.reshape(local, -1, 128), b_cols.reshape(local, -1, 128)], axis=1)
    picked = fetch_factors(packed, tile_ids, local)
    grad_rows = gather_tp(grad_out)

    fac_a = picked[:, :a_len].reshape(tiles, feats, rank_two)
    fac_b = picked[:, a_len:].reshape(tiles, rank_two, kv_dev)

    tok_t = tokens.reshape(tiles, tile_rows, feats)
    act_part = jnp.einsum("tre,tek->trk", tok_t, fac_a, preferred_element_type=f32)

    g_t = grad_rows.reshape(tiles, tile_rows, 2 * kv_width)
    g_key = lax.dynamic_slice_in_dim(g_t, col0, kv_dev, 2)
    g_val = lax.dynamic_slice_in_dim(g_t, kv_width + col0, kv_dev, 2)
    grad_part = jnp.concatenate(
        [
            jnp.einsum("trc,tkc->trk", g_key, fac_b[:, :rank_one], preferred_element_type=f32),
            jnp.einsum("trc,tkc->trk", g_val, fac_b[:, rank_one:], preferred_element_type=f32),
        ],
        axis=2,
    )
    base, fac_b = lax.optimization_barrier((jnp.dot(tokens, weight, preferred_element_type=f32), fac_b))
    base_out = reduce_scatter_tp(base)

    parts = jnp.stack([act_part, grad_part])
    flat_parts = parts.reshape(-1, 128)
    payload = jnp.concatenate([flat_parts, fac_b.astype(f32).reshape(-1, 128)])
    got = gather_axis(payload, "tp", 2)
    both = got[:, : flat_parts.shape[0]].sum(0).reshape(parts.shape)
    rank_act = both[0].astype(bf16)
    rank_grad = both[1].astype(bf16)
    full_b = got[:, flat_parts.shape[0] :].reshape(tp_count, tiles, rank_two, kv_dev)
    full_b = full_b.transpose(1, 2, 0, 3).reshape(tiles, rank_two, kv_width).astype(bf16)

    out_rows = rows // tp_count
    mine = max(1, out_rows // tile_rows)
    span = min(out_rows, tile_rows)
    first = tp_id * out_rows
    my_act = lax.dynamic_slice(rank_act, (first // tile_rows, first % tile_rows, 0), (mine, span, rank_two))
    my_b = lax.dynamic_slice(full_b, (first // tile_rows, 0, 0), (mine, rank_two, kv_width))
    lora = jnp.concatenate(
        [
            jnp.einsum("trk,tkc->trc", my_act[:, :, :rank_one], my_b[:, :rank_one], preferred_element_type=f32),
            jnp.einsum("trk,tkc->trc", my_act[:, :, rank_one:], my_b[:, rank_one:], preferred_element_type=f32),
        ],
        axis=2,
    ).reshape(out_rows, 2 * kv_width)
    key_value_output = (base_out + adapter_scale * lora).astype(bf16)

    backward = jnp.dot(grad_rows, weight.T, preferred_element_type=f32)
    adapter_back = jnp.einsum("tru,tyu->try", rank_grad, fac_a, preferred_element_type=f32)
    token_gradient = (backward + adapter_scale * adapter_back.reshape(rows, feats)).astype(bf16)

    down_grad = adapter_scale * jnp.einsum("tre,trk->tek", tok_t, rank_grad, preferred_element_type=f32)
    up_grad = adapter_scale * jnp.concatenate(
        [
            jnp.einsum("trk,trc->tkc", rank_act[:, :, :rank_one], g_key, preferred_element_type=f32),
            jnp.einsum("trk,trc->tkc", rank_act[:, :, rank_one:], g_val, preferred_element_type=f32),
        ],
        axis=1,
    )
    size_a = feats * rank_two
    flat = jnp.concatenate([down_grad.reshape(tiles, -1), up_grad.reshape(tiles, -1)], axis=1)
    summed = reduce_to_owner(flat.reshape(tiles, -1, 128), tile_ids, bank_a.shape[0]).reshape(bank_a.shape[0], -1)
    grad_a = summed[:, :size_a].reshape(bank_a.shape[0], feats, rank_two)
    grad_b = summed[:, size_a:].reshape(bank_a.shape[0], rank_two, kv_dev)
    return (key_value_output, token_gradient, grad_a, grad_b)


def solution(mesh):
    in_specs = (
        P("blk", "tp"),
        P("tp", None),
        P("blk", "tp", None),
        P("blk", None, None),
        P("blk", None),
        P(("blk", "tp"), None),
    )
    out_specs = (P(("blk", "tp"), None), P("blk", "tp"), P("blk", "tp", None), P("blk", None, "tp"))
    return jax.shard_map(
        on_device, mesh=mesh, in_specs=in_specs, out_specs=out_specs, check_vma=False
    )
```

```python
import functools

import jax
import jax.numpy as jnp
from jax import lax
from jax.experimental import pallas as pl
from jax.experimental.pallas import tpu as pltpu
from jax.sharding import PartitionSpec as P

adapter_scale = 0.5
MESH = pl.DeviceIdType.MESH


def _peer(axis, me, other, k, n):
    peer = lax.rem(me + k, n)
    return (other, peer) if axis == "tp" else (peer, other)


def _gather_kernel(axis, n, x_ref, o_ref, slots, send_sem, recv_sem):
    me = lax.axis_index(axis)
    other = lax.axis_index("blk" if axis == "tp" else "tp")
    barrier = pltpu.get_barrier_semaphore()
    for k in range(1, n):
        pl.semaphore_signal(
            barrier, inc=1, device_id=_peer(axis, me, other, k, n), device_id_type=MESH
        )
    pl.semaphore_wait(barrier, n - 1)
    sends = []
    for k in range(1, n):
        copy = pltpu.make_async_remote_copy(
            src_ref=x_ref,
            dst_ref=slots.at[me],
            send_sem=send_sem.at[k],
            recv_sem=recv_sem.at[me],
            device_id=_peer(axis, me, other, k, n),
            device_id_type=MESH,
        )
        copy.start()
        sends.append(copy)
    slots[me] = x_ref[...]
    for k in range(1, n):
        src = lax.rem(me + n - k, n)
        pltpu.make_async_remote_copy(
            src_ref=x_ref,
            dst_ref=slots.at[src],
            send_sem=send_sem.at[k],
            recv_sem=recv_sem.at[src],
            device_id=_peer(axis, me, other, n - k, n),
            device_id_type=MESH,
        ).wait_recv()
    for copy in sends:
        copy.wait_send()
    o_ref[...] = slots[...]


def gather_axis(x, axis, cid):
    n = lax.axis_size(axis)
    return pl.pallas_call(
        functools.partial(_gather_kernel, axis, n),
        out_shape=jax.ShapeDtypeStruct((n,) + x.shape, x.dtype),
        in_specs=[pl.BlockSpec(memory_space=pltpu.VMEM)],
        out_specs=pl.BlockSpec(memory_space=pltpu.VMEM),
        scratch_shapes=[
            pltpu.VMEM((n,) + x.shape, x.dtype),
            pltpu.SemaphoreType.DMA((n,)),
            pltpu.SemaphoreType.DMA((n,)),
        ],
        compiler_params=pltpu.CompilerParams(collective_id=cid, has_side_effects=True),
    )(x)


def _swap(x, bit, count):
    return lax.ppermute(x, "blk", [(i, i ^ bit) for i in range(count)])


def reduce_to_owner(rows, ids, per):
    count = lax.axis_size("blk")
    me = lax.axis_index("blk")
    nbits = count.bit_length() - 1
    order = [count // 2] + [1 << k for k in range(nbits - 1)]
    sparse = min(2, nbits)
    for bit in order[:sparse]:
        rows = jnp.concatenate([rows, _swap(rows, bit, count)])
        ids = jnp.concatenate([ids, _swap(ids, bit, count)])
        owner = ids // per
        ids = jnp.where((ids >= 0) & ((owner & bit) == (me & bit)), ids, -1)
    rest = order[sparse:]
    owner = ids // per
    slot = ids % per
    for k, bit in enumerate(rest):
        slot = slot + ((owner & bit) != 0).astype(jnp.int32) * (per << (len(rest) - 1 - k))
    hit = (slot[:, None] == jnp.arange(per << len(rest))[None, :]) & (ids >= 0)[:, None]
    dense = jnp.sum(jnp.where(hit[:, :, None, None], rows[:, None], 0.0), axis=0)
    for bit in rest:
        half = dense.shape[0] // 2
        upper = (me & bit) != 0
        keep = jnp.where(upper, dense[half:], dense[:half])
        send = jnp.where(upper, dense[:half], dense[half:])
        dense = keep + _swap(send, bit, count)
    return dense


def gather_tp(x):
    count = lax.axis_size("tp")
    me = lax.axis_index("tp")
    held = x[None]
    bit = count // 2
    while bit:
        got = lax.ppermute(held, "tp", [(i, i ^ bit) for i in range(count)])
        upper = (me & bit) != 0
        held = jnp.where(upper, jnp.stack([got, held], axis=1), jnp.stack([held, got], axis=1))
        held = held.reshape((-1,) + x.shape)
        bit //= 2
    return held.reshape((-1,) + x.shape[1:])


def reduce_scatter_tp(x, order):
    count = lax.axis_size("tp")
    me = lax.axis_index("tp")
    nbits = count.bit_length() - 1
    held = x.reshape((2,) * nbits + (x.shape[0] // count,) + x.shape[1:])
    left = [1 << (nbits - 1 - k) for k in range(nbits)]
    for bit in order:
        axis = left.index(bit)
        left.remove(bit)
        low = lax.index_in_dim(held, 0, axis, keepdims=False)
        high = lax.index_in_dim(held, 1, axis, keepdims=False)
        upper = (me & bit) != 0
        keep = jnp.where(upper, high, low)
        send = jnp.where(upper, low, high)
        held = keep + lax.ppermute(send, "tp", [(i, i ^ bit) for i in range(count)])
    return held


def fetch_factors(rows, ids, per):
    count = lax.axis_size("blk")
    me = lax.axis_index("blk")
    nbits = count.bit_length() - 1
    order = [count // 2] + [1 << k for k in range(nbits - 1)]
    far, near = order[0], order[1]
    dense = order[2:][::-1]
    held = rows
    for bit in dense:
        got = _swap(held, bit, count)
        upper = (me & bit) != 0
        held = jnp.where(upper, jnp.concatenate([got, held]), jnp.concatenate([held, got]))
    group = far | near

    def lookup(want):
        owner = want // per
        k = want % per
        for i, bit in enumerate(dense):
            k = k + ((owner & bit) != 0).astype(jnp.int32) * (per << i)
        mine = (owner & group) == (me & group)
        found = jnp.take(held, k, axis=0)
        return mine, found, owner

    pair_ids = jnp.concatenate([ids, _swap(ids, far, count)])
    their_ids = _swap(pair_ids, near, count)
    mine, found, _ = lookup(their_ids)
    sent = jnp.where(mine[:, None, None], found, jnp.zeros_like(found))
    got = _swap(sent, near, count)
    mine, found, owner = lookup(pair_ids)
    side = (owner & far) == (me & far)
    cand = jnp.where(mine[:, None, None], found, got)
    half = ids.shape[0]
    got = _swap(cand[half:], far, count)
    return jnp.where(side[:half, None, None], cand[:half], got)


def on_device(tokens, weight, bank_a, bank_b, tile_map, grad_out):
    f32, bf16 = jnp.float32, jnp.bfloat16
    tile_ids = tile_map[:, 0]
    rows, feats = tokens.shape
    tiles = tile_ids.shape[0]
    tile_rows = rows // tiles
    rank_two = bank_a.shape[2]
    rank_one = rank_two // 2
    kv_width = bank_b.shape[2]
    tp_count = lax.axis_size("tp")
    tp_id = lax.axis_index("tp")
    kv_dev = kv_width // tp_count
    col0 = tp_id * kv_dev

    b_cols = lax.dynamic_slice_in_dim(bank_b, col0, kv_dev, 2)
    local = bank_a.shape[0]
    a_len = feats * rank_two // 128
    packed = jnp.concatenate([bank_a.reshape(local, -1, 128), b_cols.reshape(local, -1, 128)], axis=1)
    picked = fetch_factors(packed, tile_ids, local)
    grad_rows = gather_tp(grad_out)

    fac_a = picked[:, :a_len].reshape(tiles, feats, rank_two)
    fac_b = picked[:, a_len:].reshape(tiles, rank_two, kv_dev)

    tok_t = tokens.reshape(tiles, tile_rows, feats)
    act_part = jnp.einsum("tre,tek->trk", tok_t, fac_a, preferred_element_type=f32)

    g_t = grad_rows.reshape(tiles, tile_rows, 2 * kv_width)
    g_key = lax.dynamic_slice_in_dim(g_t, col0, kv_dev, 2)
    g_val = lax.dynamic_slice_in_dim(g_t, kv_width + col0, kv_dev, 2)
    grad_part = jnp.concatenate(
        [
            jnp.einsum("trc,tkc->trk", g_key, fac_b[:, :rank_one], preferred_element_type=f32),
            jnp.einsum("trc,tkc->trk", g_val, fac_b[:, rank_one:], preferred_element_type=f32),
        ],
        axis=2,
    )
    base, fac_b = lax.optimization_barrier((jnp.dot(tokens, weight, preferred_element_type=f32), fac_b))
    bits = [1 << k for k in range(tp_count.bit_length() - 1)]
    half = base.shape[1] // 2
    base_out = jnp.concatenate(
        [reduce_scatter_tp(base[:, :half], bits), reduce_scatter_tp(base[:, half:], bits[::-1])], axis=1
    )

    parts = jnp.stack([act_part, grad_part])
    flat_parts = parts.reshape(-1, 128)
    payload = jnp.concatenate([flat_parts, fac_b.astype(f32).reshape(-1, 128)])
    got = gather_axis(payload, "tp", 2)
    both = got[:, : flat_parts.shape[0]].sum(0).reshape(parts.shape)
    rank_act = both[0].astype(bf16)
    rank_grad = both[1].astype(bf16)
    full_b = got[:, flat_parts.shape[0] :].reshape(tp_count, tiles, rank_two, kv_dev)
    full_b = full_b.transpose(1, 2, 0, 3).reshape(tiles, rank_two, kv_width).astype(bf16)

    out_rows = rows // tp_count
    mine = max(1, out_rows // tile_rows)
    span = min(out_rows, tile_rows)
    first = tp_id * out_rows
    my_act = lax.dynamic_slice(rank_act, (first // tile_rows, first % tile_rows, 0), (mine, span, rank_two))
    my_b = lax.dynamic_slice(full_b, (first // tile_rows, 0, 0), (mine, rank_two, kv_width))
    lora = jnp.concatenate(
        [
            jnp.einsum("trk,tkc->trc", my_act[:, :, :rank_one], my_b[:, :rank_one], preferred_element_type=f32),
            jnp.einsum("trk,tkc->trc", my_act[:, :, rank_one:], my_b[:, rank_one:], preferred_element_type=f32),
        ],
        axis=2,
    ).reshape(out_rows, 2 * kv_width)
    key_value_output = (base_out + adapter_scale * lora).astype(bf16)

    backward = jnp.dot(grad_rows, weight.T, preferred_element_type=f32)
    adapter_back = jnp.einsum("tru,tyu->try", rank_grad, fac_a, preferred_element_type=f32)
    token_gradient = (backward + adapter_scale * adapter_back.reshape(rows, feats)).astype(bf16)

    down_grad = adapter_scale * jnp.einsum("tre,trk->tek", tok_t, rank_grad, preferred_element_type=f32)
    up_grad = adapter_scale * jnp.concatenate(
        [
            jnp.einsum("trk,trc->tkc", rank_act[:, :, :rank_one], g_key, preferred_element_type=f32),
            jnp.einsum("trk,trc->tkc", rank_act[:, :, rank_one:], g_val, preferred_element_type=f32),
        ],
        axis=1,
    )
    size_a = feats * rank_two
    flat = jnp.concatenate([down_grad.reshape(tiles, -1), up_grad.reshape(tiles, -1)], axis=1)
    summed = reduce_to_owner(flat.reshape(tiles, -1, 128), tile_ids, bank_a.shape[0]).reshape(bank_a.shape[0], -1)
    grad_a = summed[:, :size_a].reshape(bank_a.shape[0], feats, rank_two)
    grad_b = summed[:, size_a:].reshape(bank_a.shape[0], rank_two, kv_dev)
    return (key_value_output, token_gradient, grad_a, grad_b)


def solution(mesh):
    in_specs = (
        P("blk", "tp"),
        P("tp", None),
        P("blk", "tp", None),
        P("blk", None, None),
        P("blk", None),
        P(("blk", "tp"), None),
    )
    out_specs = (P(("blk", "tp"), None), P("blk", "tp"), P("blk", "tp", None), P("blk", None, "tp"))
    return jax.shard_map(
        on_device, mesh=mesh, in_specs=in_specs, out_specs=out_specs, check_vma=False
    )
```

```python
import functools

import jax
import jax.numpy as jnp
from jax import lax
from jax.experimental import pallas as pl
from jax.experimental.pallas import tpu as pltpu
from jax.sharding import PartitionSpec as P

adapter_scale = 0.5
MESH = pl.DeviceIdType.MESH


def _peer(axis, me, other, k, n):
    peer = lax.rem(me + k, n)
    return (other, peer) if axis == "tp" else (peer, other)


def _gather_kernel(axis, n, x_ref, o_ref, slots, send_sem, recv_sem):
    me = lax.axis_index(axis)
    other = lax.axis_index("blk" if axis == "tp" else "tp")
    barrier = pltpu.get_barrier_semaphore()
    for k in range(1, n):
        pl.semaphore_signal(
            barrier, inc=1, device_id=_peer(axis, me, other, k, n), device_id_type=MESH
        )
    pl.semaphore_wait(barrier, n - 1)
    sends = []
    for k in range(1, n):
        copy = pltpu.make_async_remote_copy(
            src_ref=x_ref,
            dst_ref=slots.at[me],
            send_sem=send_sem.at[k],
            recv_sem=recv_sem.at[me],
            device_id=_peer(axis, me, other, k, n),
            device_id_type=MESH,
        )
        copy.start()
        sends.append(copy)
    slots[me] = x_ref[...]
    for k in range(1, n):
        src = lax.rem(me + n - k, n)
        pltpu.make_async_remote_copy(
            src_ref=x_ref,
            dst_ref=slots.at[src],
            send_sem=send_sem.at[k],
            recv_sem=recv_sem.at[src],
            device_id=_peer(axis, me, other, n - k, n),
            device_id_type=MESH,
        ).wait_recv()
    for copy in sends:
        copy.wait_send()
    o_ref[...] = slots[...]


def gather_axis(x, axis, cid):
    n = lax.axis_size(axis)
    return pl.pallas_call(
        functools.partial(_gather_kernel, axis, n),
        out_shape=jax.ShapeDtypeStruct((n,) + x.shape, x.dtype),
        in_specs=[pl.BlockSpec(memory_space=pltpu.VMEM)],
        out_specs=pl.BlockSpec(memory_space=pltpu.VMEM),
        scratch_shapes=[
            pltpu.VMEM((n,) + x.shape, x.dtype),
            pltpu.SemaphoreType.DMA((n,)),
            pltpu.SemaphoreType.DMA((n,)),
        ],
        compiler_params=pltpu.CompilerParams(collective_id=cid, has_side_effects=True),
    )(x)


def _swap(x, bit, count):
    return lax.ppermute(x, "blk", [(i, i ^ bit) for i in range(count)])


def reduce_to_owner(rows, ids, per):
    count = lax.axis_size("blk")
    me = lax.axis_index("blk")
    nbits = count.bit_length() - 1
    order = [count // 2] + [1 << k for k in range(nbits - 1)]
    sparse = min(2, nbits)
    for bit in order[:sparse]:
        rows = jnp.concatenate([rows, _swap(rows, bit, count)])
        ids = jnp.concatenate([ids, _swap(ids, bit, count)])
        owner = ids // per
        ids = jnp.where((ids >= 0) & ((owner & bit) == (me & bit)), ids, -1)
    rest = order[sparse:]
    owner = ids // per
    slot = ids % per
    for k, bit in enumerate(rest):
        slot = slot + ((owner & bit) != 0).astype(jnp.int32) * (per << (len(rest) - 1 - k))
    hit = (slot[:, None] == jnp.arange(per << len(rest))[None, :]) & (ids >= 0)[:, None]
    dense = jnp.sum(jnp.where(hit[:, :, None, None], rows[:, None], 0.0), axis=0)
    for bit in rest:
        half = dense.shape[0] // 2
        upper = (me & bit) != 0
        keep = jnp.where(upper, dense[half:], dense[:half])
        send = jnp.where(upper, dense[:half], dense[half:])
        dense = keep + _swap(send, bit, count)
    return dense


def gather_tp(x):
    count = lax.axis_size("tp")
    me = lax.axis_index("tp")
    held = x[None]
    bit = count // 2
    while bit:
        got = lax.ppermute(held, "tp", [(i, i ^ bit) for i in range(count)])
        upper = (me & bit) != 0
        held = jnp.where(upper, jnp.stack([got, held], axis=1), jnp.stack([held, got], axis=1))
        held = held.reshape((-1,) + x.shape)
        bit //= 2
    return held.reshape((-1,) + x.shape[1:])


def reduce_scatter_tp(x, order):
    count = lax.axis_size("tp")
    me = lax.axis_index("tp")
    nbits = count.bit_length() - 1
    held = x.reshape((2,) * nbits + (x.shape[0] // count,) + x.shape[1:])
    left = [1 << (nbits - 1 - k) for k in range(nbits)]
    for bit in order:
        axis = left.index(bit)
        left.remove(bit)
        low = lax.index_in_dim(held, 0, axis, keepdims=False)
        high = lax.index_in_dim(held, 1, axis, keepdims=False)
        upper = (me & bit) != 0
        keep = jnp.where(upper, high, low)
        send = jnp.where(upper, low, high)
        held = keep + lax.ppermute(send, "tp", [(i, i ^ bit) for i in range(count)])
    return held


def fetch_factors(rows, ids, per):
    count = lax.axis_size("blk")
    me = lax.axis_index("blk")
    nbits = count.bit_length() - 1
    order = [count // 2] + [1 << k for k in range(nbits - 1)]
    far, near = order[0], order[1]
    dense = order[2:][::-1]
    held = rows
    for bit in dense:
        got = _swap(held, bit, count)
        upper = (me & bit) != 0
        held = jnp.where(upper, jnp.concatenate([got, held]), jnp.concatenate([held, got]))
    group = far | near

    def lookup(want):
        owner = want // per
        k = want % per
        for i, bit in enumerate(dense):
            k = k + ((owner & bit) != 0).astype(jnp.int32) * (per << i)
        mine = (owner & group) == (me & group)
        found = jnp.take(held, k, axis=0)
        return mine, found, owner

    pair_ids = jnp.concatenate([ids, _swap(ids, far, count)])
    their_ids = _swap(pair_ids, near, count)
    mine, found, _ = lookup(their_ids)
    sent = jnp.where(mine[:, None, None], found, jnp.zeros_like(found))
    got = _swap(sent, near, count)
    mine, found, owner = lookup(pair_ids)
    side = (owner & far) == (me & far)
    cand = jnp.where(mine[:, None, None], found, got)
    half = ids.shape[0]
    got = _swap(cand[half:], far, count)
    return jnp.where(side[:half, None, None], cand[:half], got)


def on_device(tokens, weight, bank_a, bank_b, tile_map, grad_out):
    f32, bf16 = jnp.float32, jnp.bfloat16
    tile_ids = tile_map[:, 0]
    rows, feats = tokens.shape
    tiles = tile_ids.shape[0]
    tile_rows = rows // tiles
    rank_two = bank_a.shape[2]
    rank_one = rank_two // 2
    kv_width = bank_b.shape[2]
    tp_count = lax.axis_size("tp")
    tp_id = lax.axis_index("tp")
    kv_dev = kv_width // tp_count
    col0 = tp_id * kv_dev

    b_cols = lax.dynamic_slice_in_dim(bank_b, col0, kv_dev, 2)
    local = bank_a.shape[0]
    a_len = feats * rank_two // 128
    packed = jnp.concatenate([bank_a.reshape(local, -1, 128), b_cols.reshape(local, -1, 128)], axis=1)
    picked = fetch_factors(packed, tile_ids, local)
    grad_rows = gather_tp(grad_out)

    fac_a = picked[:, :a_len].reshape(tiles, feats, rank_two)
    fac_b = picked[:, a_len:].reshape(tiles, rank_two, kv_dev)

    tok_t = tokens.reshape(tiles, tile_rows, feats)
    act_part = jnp.einsum("tre,tek->trk", tok_t, fac_a, preferred_element_type=f32)

    g_t = grad_rows.reshape(tiles, tile_rows, 2 * kv_width)
    g_key = lax.dynamic_slice_in_dim(g_t, col0, kv_dev, 2)
    g_val = lax.dynamic_slice_in_dim(g_t, kv_width + col0, kv_dev, 2)
    grad_part = jnp.concatenate(
        [
            jnp.einsum("trc,tkc->trk", g_key, fac_b[:, :rank_one], preferred_element_type=f32),
            jnp.einsum("trc,tkc->trk", g_val, fac_b[:, rank_one:], preferred_element_type=f32),
        ],
        axis=2,
    )
    base, fac_b = lax.optimization_barrier((jnp.dot(tokens, weight, preferred_element_type=f32), fac_b))
    bits = [1 << k for k in range(tp_count.bit_length() - 1)]
    half = base.shape[1] // 2
    base_out = jnp.concatenate(
        [reduce_scatter_tp(base[:, :half], bits), reduce_scatter_tp(base[:, half:], bits[1::-1] + bits[2:])], axis=1
    )

    parts = jnp.stack([act_part, grad_part])
    flat_parts = parts.reshape(-1, 128)
    payload = jnp.concatenate([flat_parts, fac_b.astype(f32).reshape(-1, 128)])
    got = gather_axis(payload, "tp", 2)
    both = got[:, : flat_parts.shape[0]].sum(0).reshape(parts.shape)
    rank_act = both[0].astype(bf16)
    rank_grad = both[1].astype(bf16)
    full_b = got[:, flat_parts.shape[0] :].reshape(tp_count, tiles, rank_two, kv_dev)
    full_b = full_b.transpose(1, 2, 0, 3).reshape(tiles, rank_two, kv_width).astype(bf16)

    out_rows = rows // tp_count
    mine = max(1, out_rows // tile_rows)
    span = min(out_rows, tile_rows)
    first = tp_id * out_rows
    my_act = lax.dynamic_slice(rank_act, (first // tile_rows, first % tile_rows, 0), (mine, span, rank_two))
    my_b = lax.dynamic_slice(full_b, (first // tile_rows, 0, 0), (mine, rank_two, kv_width))
    lora = jnp.concatenate(
        [
            jnp.einsum("trk,tkc->trc", my_act[:, :, :rank_one], my_b[:, :rank_one], preferred_element_type=f32),
            jnp.einsum("trk,tkc->trc", my_act[:, :, rank_one:], my_b[:, rank_one:], preferred_element_type=f32),
        ],
        axis=2,
    ).reshape(out_rows, 2 * kv_width)
    key_value_output = (base_out + adapter_scale * lora).astype(bf16)

    backward = jnp.dot(grad_rows, weight.T, preferred_element_type=f32)
    adapter_back = jnp.einsum("tru,tyu->try", rank_grad, fac_a, preferred_element_type=f32)
    token_gradient = (backward + adapter_scale * adapter_back.reshape(rows, feats)).astype(bf16)

    down_grad = adapter_scale * jnp.einsum("tre,trk->tek", tok_t, rank_grad, preferred_element_type=f32)
    up_grad = adapter_scale * jnp.concatenate(
        [
            jnp.einsum("trk,trc->tkc", rank_act[:, :, :rank_one], g_key, preferred_element_type=f32),
            jnp.einsum("trk,trc->tkc", rank_act[:, :, rank_one:], g_val, preferred_element_type=f32),
        ],
        axis=1,
    )
    size_a = feats * rank_two
    flat = jnp.concatenate([down_grad.reshape(tiles, -1), up_grad.reshape(tiles, -1)], axis=1)
    summed = reduce_to_owner(flat.reshape(tiles, -1, 128), tile_ids, bank_a.shape[0]).reshape(bank_a.shape[0], -1)
    grad_a = summed[:, :size_a].reshape(bank_a.shape[0], feats, rank_two)
    grad_b = summed[:, size_a:].reshape(bank_a.shape[0], rank_two, kv_dev)
    return (key_value_output, token_gradient, grad_a, grad_b)


def solution(mesh):
    in_specs = (
        P("blk", "tp"),
        P("tp", None),
        P("blk", "tp", None),
        P("blk", None, None),
        P("blk", None),
        P(("blk", "tp"), None),
    )
    out_specs = (P(("blk", "tp"), None), P("blk", "tp"), P("blk", "tp", None), P("blk", None, "tp"))
    return jax.shard_map(
        on_device, mesh=mesh, in_specs=in_specs, out_specs=out_specs, check_vma=False
    )
```

```python
import functools

import jax
import jax.numpy as jnp
from jax import lax
from jax.experimental import pallas as pl
from jax.experimental.pallas import tpu as pltpu
from jax.sharding import PartitionSpec as P

adapter_scale = 0.5
MESH = pl.DeviceIdType.MESH


def _peer(axis, me, other, k, n):
    peer = lax.rem(me + k, n)
    return (other, peer) if axis == "tp" else (peer, other)


def _gather_kernel(axis, n, x_ref, o_ref, slots, send_sem, recv_sem):
    me = lax.axis_index(axis)
    other = lax.axis_index("blk" if axis == "tp" else "tp")
    barrier = pltpu.get_barrier_semaphore()
    for k in range(1, n):
        pl.semaphore_signal(
            barrier, inc=1, device_id=_peer(axis, me, other, k, n), device_id_type=MESH
        )
    pl.semaphore_wait(barrier, n - 1)
    sends = []
    for k in range(1, n):
        copy = pltpu.make_async_remote_copy(
            src_ref=x_ref,
            dst_ref=slots.at[me],
            send_sem=send_sem.at[k],
            recv_sem=recv_sem.at[me],
            device_id=_peer(axis, me, other, k, n),
            device_id_type=MESH,
        )
        copy.start()
        sends.append(copy)
    slots[me] = x_ref[...]
    for k in range(1, n):
        src = lax.rem(me + n - k, n)
        pltpu.make_async_remote_copy(
            src_ref=x_ref,
            dst_ref=slots.at[src],
            send_sem=send_sem.at[k],
            recv_sem=recv_sem.at[src],
            device_id=_peer(axis, me, other, n - k, n),
            device_id_type=MESH,
        ).wait_recv()
    for copy in sends:
        copy.wait_send()
    o_ref[...] = slots[...]


def gather_axis(x, axis, cid):
    n = lax.axis_size(axis)
    return pl.pallas_call(
        functools.partial(_gather_kernel, axis, n),
        out_shape=jax.ShapeDtypeStruct((n,) + x.shape, x.dtype),
        in_specs=[pl.BlockSpec(memory_space=pltpu.VMEM)],
        out_specs=pl.BlockSpec(memory_space=pltpu.VMEM),
        scratch_shapes=[
            pltpu.VMEM((n,) + x.shape, x.dtype),
            pltpu.SemaphoreType.DMA((n,)),
            pltpu.SemaphoreType.DMA((n,)),
        ],
        compiler_params=pltpu.CompilerParams(collective_id=cid, has_side_effects=True),
    )(x)


def _swap(x, bit, count):
    return lax.ppermute(x, "blk", [(i, i ^ bit) for i in range(count)])


def reduce_to_owner(rows, ids, per):
    count = lax.axis_size("blk")
    me = lax.axis_index("blk")
    nbits = count.bit_length() - 1
    order = [count // 2] + [1 << k for k in range(nbits - 1)]
    sparse = min(2, nbits)
    for bit in order[:sparse]:
        rows = jnp.concatenate([rows, _swap(rows, bit, count)])
        ids = jnp.concatenate([ids, _swap(ids, bit, count)])
        owner = ids // per
        ids = jnp.where((ids >= 0) & ((owner & bit) == (me & bit)), ids, -1)
    rest = order[sparse:]
    owner = ids // per
    slot = ids % per
    for k, bit in enumerate(rest):
        slot = slot + ((owner & bit) != 0).astype(jnp.int32) * (per << (len(rest) - 1 - k))
    hit = (slot[:, None] == jnp.arange(per << len(rest))[None, :]) & (ids >= 0)[:, None]
    dense = jnp.sum(jnp.where(hit[:, :, None, None], rows[:, None], 0.0), axis=0)
    for bit in rest:
        half = dense.shape[0] // 2
        upper = (me & bit) != 0
        keep = jnp.where(upper, dense[half:], dense[:half])
        send = jnp.where(upper, dense[:half], dense[half:])
        dense = keep + _swap(send, bit, count)
    return dense


def gather_tp(x):
    count = lax.axis_size("tp")
    me = lax.axis_index("tp")
    held = x[None]
    bit = count // 2
    while bit:
        got = lax.ppermute(held, "tp", [(i, i ^ bit) for i in range(count)])
        upper = (me & bit) != 0
        held = jnp.where(upper, jnp.stack([got, held], axis=1), jnp.stack([held, got], axis=1))
        held = held.reshape((-1,) + x.shape)
        bit //= 2
    return held.reshape((-1,) + x.shape[1:])


def reduce_scatter_tp(x, tie):
    count = lax.axis_size("tp")
    me = lax.axis_index("tp")
    nbits = count.bit_length() - 1
    held = x.reshape((2,) * nbits + (x.shape[0] // count,) + x.shape[1:])
    for k in range(nbits):
        bit = 1 << k
        axis = nbits - 1 - k
        low = lax.index_in_dim(held, 0, axis, keepdims=False)
        high = lax.index_in_dim(held, 1, axis, keepdims=False)
        upper = (me & bit) != 0
        keep = jnp.where(upper, high, low)
        send = jnp.where(upper, low, high)
        held = keep + lax.ppermute(send, "tp", [(i, i ^ bit) for i in range(count)])
        if k == 0:
            held, tie = lax.optimization_barrier((held, tie))
    return held, tie


def fetch_factors(rows, ids, per):
    count = lax.axis_size("blk")
    me = lax.axis_index("blk")
    nbits = count.bit_length() - 1
    order = [count // 2] + [1 << k for k in range(nbits - 1)]
    far, near = order[0], order[1]
    dense = order[2:][::-1]
    held = rows
    for bit in dense:
        got = _swap(held, bit, count)
        upper = (me & bit) != 0
        held = jnp.where(upper, jnp.concatenate([got, held]), jnp.concatenate([held, got]))
    group = far | near

    def lookup(want):
        owner = want // per
        k = want % per
        for i, bit in enumerate(dense):
            k = k + ((owner & bit) != 0).astype(jnp.int32) * (per << i)
        mine = (owner & group) == (me & group)
        found = jnp.take(held, k, axis=0)
        return mine, found, owner

    pair_ids = jnp.concatenate([ids, _swap(ids, far, count)])
    their_ids = _swap(pair_ids, near, count)
    mine, found, _ = lookup(their_ids)
    sent = jnp.where(mine[:, None, None], found, jnp.zeros_like(found))
    got = _swap(sent, near, count)
    mine, found, owner = lookup(pair_ids)
    side = (owner & far) == (me & far)
    cand = jnp.where(mine[:, None, None], found, got)
    half = ids.shape[0]
    got = _swap(cand[half:], far, count)
    return jnp.where(side[:half, None, None], cand[:half], got)


def on_device(tokens, weight, bank_a, bank_b, tile_map, grad_out):
    f32, bf16 = jnp.float32, jnp.bfloat16
    tile_ids = tile_map[:, 0]
    rows, feats = tokens.shape
    tiles = tile_ids.shape[0]
    tile_rows = rows // tiles
    rank_two = bank_a.shape[2]
    rank_one = rank_two // 2
    kv_width = bank_b.shape[2]
    tp_count = lax.axis_size("tp")
    tp_id = lax.axis_index("tp")
    kv_dev = kv_width // tp_count
    col0 = tp_id * kv_dev

    b_cols = lax.dynamic_slice_in_dim(bank_b, col0, kv_dev, 2)
    local = bank_a.shape[0]
    a_len = feats * rank_two // 128
    packed = jnp.concatenate([bank_a.reshape(local, -1, 128), b_cols.reshape(local, -1, 128)], axis=1)
    picked = fetch_factors(packed, tile_ids, local)
    grad_rows = gather_tp(grad_out)

    fac_a = picked[:, :a_len].reshape(tiles, feats, rank_two)
    fac_b = picked[:, a_len:].reshape(tiles, rank_two, kv_dev)

    tok_t = tokens.reshape(tiles, tile_rows, feats)
    act_part = jnp.einsum("tre,tek->trk", tok_t, fac_a, preferred_element_type=f32)

    g_t = grad_rows.reshape(tiles, tile_rows, 2 * kv_width)
    g_key = lax.dynamic_slice_in_dim(g_t, col0, kv_dev, 2)
    g_val = lax.dynamic_slice_in_dim(g_t, kv_width + col0, kv_dev, 2)
    grad_part = jnp.concatenate(
        [
            jnp.einsum("trc,tkc->trk", g_key, fac_b[:, :rank_one], preferred_element_type=f32),
            jnp.einsum("trc,tkc->trk", g_val, fac_b[:, rank_one:], preferred_element_type=f32),
        ],
        axis=2,
    )
    parts = jnp.stack([act_part, grad_part])
    flat_parts = parts.reshape(-1, 128)
    payload = jnp.concatenate([flat_parts, fac_b.astype(f32).reshape(-1, 128)])
    got = gather_axis(payload, "tp", 2)
    both = got[:, : flat_parts.shape[0]].sum(0).reshape(parts.shape)
    rank_act = both[0].astype(bf16)
    rank_grad = both[1].astype(bf16)
    full_b = got[:, flat_parts.shape[0] :].reshape(tp_count, tiles, rank_two, kv_dev)
    full_b = full_b.transpose(1, 2, 0, 3).reshape(tiles, rank_two, kv_width).astype(bf16)

    out_rows = rows // tp_count
    mine = max(1, out_rows // tile_rows)
    span = min(out_rows, tile_rows)
    first = tp_id * out_rows
    my_act = lax.dynamic_slice(rank_act, (first // tile_rows, first % tile_rows, 0), (mine, span, rank_two))
    my_b = lax.dynamic_slice(full_b, (first // tile_rows, 0, 0), (mine, rank_two, kv_width))
    lora = jnp.concatenate(
        [
            jnp.einsum("trk,tkc->trc", my_act[:, :, :rank_one], my_b[:, :rank_one], preferred_element_type=f32),
            jnp.einsum("trk,tkc->trc", my_act[:, :, rank_one:], my_b[:, rank_one:], preferred_element_type=f32),
        ],
        axis=2,
    ).reshape(out_rows, 2 * kv_width)

    backward = jnp.dot(grad_rows, weight.T, preferred_element_type=f32)
    adapter_back = jnp.einsum("tru,tyu->try", rank_grad, fac_a, preferred_element_type=f32)
    token_gradient = (backward + adapter_scale * adapter_back.reshape(rows, feats)).astype(bf16)

    down_grad = adapter_scale * jnp.einsum("tre,trk->tek", tok_t, rank_grad, preferred_element_type=f32)
    up_grad = adapter_scale * jnp.concatenate(
        [
            jnp.einsum("trk,trc->tkc", rank_act[:, :, :rank_one], g_key, preferred_element_type=f32),
            jnp.einsum("trk,trc->tkc", rank_act[:, :, rank_one:], g_val, preferred_element_type=f32),
        ],
        axis=1,
    )
    size_a = feats * rank_two
    flat = jnp.concatenate([down_grad.reshape(tiles, -1), up_grad.reshape(tiles, -1)], axis=1)
    base, fac_b = lax.optimization_barrier((jnp.dot(tokens, weight, preferred_element_type=f32), fac_b))

    base_out, flat = reduce_scatter_tp(base, flat)
    key_value_output = (base_out + adapter_scale * lora).astype(bf16)
    summed = reduce_to_owner(flat.reshape(tiles, -1, 128), tile_ids, bank_a.shape[0]).reshape(bank_a.shape[0], -1)
    grad_a = summed[:, :size_a].reshape(bank_a.shape[0], feats, rank_two)
    grad_b = summed[:, size_a:].reshape(bank_a.shape[0], rank_two, kv_dev)
    return (key_value_output, token_gradient, grad_a, grad_b)


def solution(mesh):
    in_specs = (
        P("blk", "tp"),
        P("tp", None),
        P("blk", "tp", None),
        P("blk", None, None),
        P("blk", None),
        P(("blk", "tp"), None),
    )
    out_specs = (P(("blk", "tp"), None), P("blk", "tp"), P("blk", "tp", None), P("blk", None, "tp"))
    return jax.shard_map(
        on_device, mesh=mesh, in_specs=in_specs, out_specs=out_specs, check_vma=False
    )
```

```python
import functools

import jax
import jax.numpy as jnp
from jax import lax
from jax.experimental import pallas as pl
from jax.experimental.pallas import tpu as pltpu
from jax.sharding import PartitionSpec as P

adapter_scale = 0.5
MESH = pl.DeviceIdType.MESH


def _peer(axis, me, other, k, n):
    peer = lax.rem(me + k, n)
    return (other, peer) if axis == "tp" else (peer, other)


def _gather_kernel(axis, n, x_ref, o_ref, slots, send_sem, recv_sem):
    me = lax.axis_index(axis)
    other = lax.axis_index("blk" if axis == "tp" else "tp")
    barrier = pltpu.get_barrier_semaphore()
    for k in range(1, n):
        pl.semaphore_signal(
            barrier, inc=1, device_id=_peer(axis, me, other, k, n), device_id_type=MESH
        )
    pl.semaphore_wait(barrier, n - 1)
    sends = []
    for k in range(1, n):
        copy = pltpu.make_async_remote_copy(
            src_ref=x_ref,
            dst_ref=slots.at[me],
            send_sem=send_sem.at[k],
            recv_sem=recv_sem.at[me],
            device_id=_peer(axis, me, other, k, n),
            device_id_type=MESH,
        )
        copy.start()
        sends.append(copy)
    slots[me] = x_ref[...]
    for k in range(1, n):
        src = lax.rem(me + n - k, n)
        pltpu.make_async_remote_copy(
            src_ref=x_ref,
            dst_ref=slots.at[src],
            send_sem=send_sem.at[k],
            recv_sem=recv_sem.at[src],
            device_id=_peer(axis, me, other, n - k, n),
            device_id_type=MESH,
        ).wait_recv()
    for copy in sends:
        copy.wait_send()
    o_ref[...] = slots[...]


def gather_axis(x, axis, cid):
    n = lax.axis_size(axis)
    return pl.pallas_call(
        functools.partial(_gather_kernel, axis, n),
        out_shape=jax.ShapeDtypeStruct((n,) + x.shape, x.dtype),
        in_specs=[pl.BlockSpec(memory_space=pltpu.VMEM)],
        out_specs=pl.BlockSpec(memory_space=pltpu.VMEM),
        scratch_shapes=[
            pltpu.VMEM((n,) + x.shape, x.dtype),
            pltpu.SemaphoreType.DMA((n,)),
            pltpu.SemaphoreType.DMA((n,)),
        ],
        compiler_params=pltpu.CompilerParams(collective_id=cid, has_side_effects=True),
    )(x)


def _swap(x, bit, count):
    return lax.ppermute(x, "blk", [(i, i ^ bit) for i in range(count)])


def reduce_to_owner(rows, ids, per):
    count = lax.axis_size("blk")
    me = lax.axis_index("blk")
    nbits = count.bit_length() - 1
    order = [count // 2] + [1 << k for k in range(nbits - 1)]
    sparse = min(2, nbits)
    for bit in order[:sparse]:
        rows = jnp.concatenate([rows, _swap(rows, bit, count)])
        ids = jnp.concatenate([ids, _swap(ids, bit, count)])
        owner = ids // per
        ids = jnp.where((ids >= 0) & ((owner & bit) == (me & bit)), ids, -1)
    rest = order[sparse:]
    owner = ids // per
    slot = ids % per
    for k, bit in enumerate(rest):
        slot = slot + ((owner & bit) != 0).astype(jnp.int32) * (per << (len(rest) - 1 - k))
    hit = (slot[:, None] == jnp.arange(per << len(rest))[None, :]) & (ids >= 0)[:, None]
    dense = jnp.sum(jnp.where(hit[:, :, None, None], rows[:, None], 0.0), axis=0)
    for bit in rest:
        half = dense.shape[0] // 2
        upper = (me & bit) != 0
        keep = jnp.where(upper, dense[half:], dense[:half])
        send = jnp.where(upper, dense[:half], dense[half:])
        dense = keep + _swap(send, bit, count)
    return dense


def gather_tp(x):
    count = lax.axis_size("tp")
    me = lax.axis_index("tp")
    held = x[None]
    bit = count // 2
    while bit:
        got = lax.ppermute(held, "tp", [(i, i ^ bit) for i in range(count)])
        upper = (me & bit) != 0
        held = jnp.where(upper, jnp.stack([got, held], axis=1), jnp.stack([held, got], axis=1))
        held = held.reshape((-1,) + x.shape)
        bit //= 2
    return held.reshape((-1,) + x.shape[1:])


def reduce_scatter_tp(x):
    count = lax.axis_size("tp")
    me = lax.axis_index("tp")
    nbits = count.bit_length() - 1
    held = x.reshape((2,) * nbits + (x.shape[0] // count,) + x.shape[1:])
    for k in range(nbits):
        bit = 1 << k
        axis = nbits - 1 - k
        low = lax.index_in_dim(held, 0, axis, keepdims=False)
        high = lax.index_in_dim(held, 1, axis, keepdims=False)
        upper = (me & bit) != 0
        keep = jnp.where(upper, high, low)
        send = jnp.where(upper, low, high)
        held = keep + lax.ppermute(send, "tp", [(i, i ^ bit) for i in range(count)])
    return held


def fetch_factors(rows, ids, per):
    count = lax.axis_size("blk")
    me = lax.axis_index("blk")
    nbits = count.bit_length() - 1
    order = [count // 2] + [1 << k for k in range(nbits - 1)]
    far, near = order[0], order[1]
    dense = order[2:][::-1]
    held = rows
    for bit in dense:
        got = _swap(held, bit, count)
        upper = (me & bit) != 0
        held = jnp.where(upper, jnp.concatenate([got, held]), jnp.concatenate([held, got]))
    group = far | near

    def lookup(want):
        owner = want // per
        k = want % per
        for i, bit in enumerate(dense):
            k = k + ((owner & bit) != 0).astype(jnp.int32) * (per << i)
        mine = (owner & group) == (me & group)
        found = jnp.take(held, k, axis=0)
        return mine, found, owner

    pair_ids = jnp.concatenate([ids, _swap(ids, far, count)])
    their_ids = _swap(pair_ids, near, count)
    mine, found, _ = lookup(their_ids)
    sent = jnp.where(mine[:, None, None], found, jnp.zeros_like(found))
    got = _swap(sent, near, count)
    mine, found, owner = lookup(pair_ids)
    side = (owner & far) == (me & far)
    cand = jnp.where(mine[:, None, None], found, got)
    half = ids.shape[0]
    got = _swap(cand[half:], far, count)
    return jnp.where(side[:half, None, None], cand[:half], got)


def on_device(tokens, weight, bank_a, bank_b, tile_map, grad_out):
    f32, bf16 = jnp.float32, jnp.bfloat16
    tile_ids = tile_map[:, 0]
    rows, feats = tokens.shape
    tiles = tile_ids.shape[0]
    tile_rows = rows // tiles
    rank_two = bank_a.shape[2]
    rank_one = rank_two // 2
    kv_width = bank_b.shape[2]
    tp_count = lax.axis_size("tp")
    tp_id = lax.axis_index("tp")
    kv_dev = kv_width // tp_count
    col0 = tp_id * kv_dev

    b_cols = lax.dynamic_slice_in_dim(bank_b, col0, kv_dev, 2)
    local = bank_a.shape[0]
    a_len = feats * rank_two // 128
    packed = jnp.concatenate([bank_a.reshape(local, -1, 128), b_cols.reshape(local, -1, 128)], axis=1)
    picked = fetch_factors(packed, tile_ids, local)
    grad_rows = gather_tp(grad_out)

    fac_a = picked[:, :a_len].reshape(tiles, feats, rank_two)
    fac_b = picked[:, a_len:].reshape(tiles, rank_two, kv_dev)

    tok_t = tokens.reshape(tiles, tile_rows, feats)
    act_part = jnp.einsum("tre,tek->trk", tok_t, fac_a, preferred_element_type=f32)

    g_t = grad_rows.reshape(tiles, tile_rows, 2 * kv_width)
    g_key = lax.dynamic_slice_in_dim(g_t, col0, kv_dev, 2)
    g_val = lax.dynamic_slice_in_dim(g_t, kv_width + col0, kv_dev, 2)
    grad_part = jnp.concatenate(
        [
            jnp.einsum("trc,tkc->trk", g_key, fac_b[:, :rank_one], preferred_element_type=f32),
            jnp.einsum("trc,tkc->trk", g_val, fac_b[:, rank_one:], preferred_element_type=f32),
        ],
        axis=2,
    )
    base, fac_b = lax.optimization_barrier((jnp.dot(tokens, weight, preferred_element_type=f32), fac_b))
    half = base.shape[1] // 2
    base_out = jnp.concatenate(
        [
            lax.psum_scatter(base[:, :half], "tp", scatter_dimension=0, tiled=True),
            reduce_scatter_tp(base[:, half:]),
        ],
        axis=1,
    )

    parts = jnp.stack([act_part, grad_part])
    flat_parts = parts.reshape(-1, 128)
    payload = jnp.concatenate([flat_parts, fac_b.astype(f32).reshape(-1, 128)])
    got = gather_axis(payload, "tp", 2)
    both = got[:, : flat_parts.shape[0]].sum(0).reshape(parts.shape)
    rank_act = both[0].astype(bf16)
    rank_grad = both[1].astype(bf16)
    full_b = got[:, flat_parts.shape[0] :].reshape(tp_count, tiles, rank_two, kv_dev)
    full_b = full_b.transpose(1, 2, 0, 3).reshape(tiles, rank_two, kv_width).astype(bf16)

    out_rows = rows // tp_count
    mine = max(1, out_rows // tile_rows)
    span = min(out_rows, tile_rows)
    first = tp_id * out_rows
    my_act = lax.dynamic_slice(rank_act, (first // tile_rows, first % tile_rows, 0), (mine, span, rank_two))
    my_b = lax.dynamic_slice(full_b, (first // tile_rows, 0, 0), (mine, rank_two, kv_width))
    lora = jnp.concatenate(
        [
            jnp.einsum("trk,tkc->trc", my_act[:, :, :rank_one], my_b[:, :rank_one], preferred_element_type=f32),
            jnp.einsum("trk,tkc->trc", my_act[:, :, rank_one:], my_b[:, rank_one:], preferred_element_type=f32),
        ],
        axis=2,
    ).reshape(out_rows, 2 * kv_width)
    key_value_output = (base_out + adapter_scale * lora).astype(bf16)

    backward = jnp.dot(grad_rows, weight.T, preferred_element_type=f32)
    adapter_back = jnp.einsum("tru,tyu->try", rank_grad, fac_a, preferred_element_type=f32)
    token_gradient = (backward + adapter_scale * adapter_back.reshape(rows, feats)).astype(bf16)

    down_grad = adapter_scale * jnp.einsum("tre,trk->tek", tok_t, rank_grad, preferred_element_type=f32)
    up_grad = adapter_scale * jnp.concatenate(
        [
            jnp.einsum("trk,trc->tkc", rank_act[:, :, :rank_one], g_key, preferred_element_type=f32),
            jnp.einsum("trk,trc->tkc", rank_act[:, :, rank_one:], g_val, preferred_element_type=f32),
        ],
        axis=1,
    )
    size_a = feats * rank_two
    flat = jnp.concatenate([down_grad.reshape(tiles, -1), up_grad.reshape(tiles, -1)], axis=1)
    summed = reduce_to_owner(flat.reshape(tiles, -1, 128), tile_ids, bank_a.shape[0]).reshape(bank_a.shape[0], -1)
    grad_a = summed[:, :size_a].reshape(bank_a.shape[0], feats, rank_two)
    grad_b = summed[:, size_a:].reshape(bank_a.shape[0], rank_two, kv_dev)
    return (key_value_output, token_gradient, grad_a, grad_b)


def solution(mesh):
    in_specs = (
        P("blk", "tp"),
        P("tp", None),
        P("blk", "tp", None),
        P("blk", None, None),
        P("blk", None),
        P(("blk", "tp"), None),
    )
    out_specs = (P(("blk", "tp"), None), P("blk", "tp"), P("blk", "tp", None), P("blk", None, "tp"))
    return jax.shard_map(
        on_device, mesh=mesh, in_specs=in_specs, out_specs=out_specs, check_vma=False
    )
```

```python
import functools

import jax
import jax.numpy as jnp
from jax import lax
from jax.experimental import pallas as pl
from jax.experimental.pallas import tpu as pltpu
from jax.sharding import PartitionSpec as P

adapter_scale = 0.5
MESH = pl.DeviceIdType.MESH


def _peer(axis, me, other, k, n):
    peer = lax.rem(me + k, n)
    return (other, peer) if axis == "tp" else (peer, other)


def _gather_kernel(axis, n, x_ref, o_ref, slots, send_sem, recv_sem):
    me = lax.axis_index(axis)
    other = lax.axis_index("blk" if axis == "tp" else "tp")
    barrier = pltpu.get_barrier_semaphore()
    for k in range(1, n):
        pl.semaphore_signal(
            barrier, inc=1, device_id=_peer(axis, me, other, k, n), device_id_type=MESH
        )
    pl.semaphore_wait(barrier, n - 1)
    sends = []
    for k in range(1, n):
        copy = pltpu.make_async_remote_copy(
            src_ref=x_ref,
            dst_ref=slots.at[me],
            send_sem=send_sem.at[k],
            recv_sem=recv_sem.at[me],
            device_id=_peer(axis, me, other, k, n),
            device_id_type=MESH,
        )
        copy.start()
        sends.append(copy)
    slots[me] = x_ref[...]
    for k in range(1, n):
        src = lax.rem(me + n - k, n)
        pltpu.make_async_remote_copy(
            src_ref=x_ref,
            dst_ref=slots.at[src],
            send_sem=send_sem.at[k],
            recv_sem=recv_sem.at[src],
            device_id=_peer(axis, me, other, n - k, n),
            device_id_type=MESH,
        ).wait_recv()
    for copy in sends:
        copy.wait_send()
    o_ref[...] = slots[...]


def gather_axis(x, axis, cid):
    n = lax.axis_size(axis)
    return pl.pallas_call(
        functools.partial(_gather_kernel, axis, n),
        out_shape=jax.ShapeDtypeStruct((n,) + x.shape, x.dtype),
        in_specs=[pl.BlockSpec(memory_space=pltpu.VMEM)],
        out_specs=pl.BlockSpec(memory_space=pltpu.VMEM),
        scratch_shapes=[
            pltpu.VMEM((n,) + x.shape, x.dtype),
            pltpu.SemaphoreType.DMA((n,)),
            pltpu.SemaphoreType.DMA((n,)),
        ],
        compiler_params=pltpu.CompilerParams(collective_id=cid, has_side_effects=True),
    )(x)


def _swap(x, bit, count):
    return lax.ppermute(x, "blk", [(i, i ^ bit) for i in range(count)])


def reduce_to_owner(rows, ids, per):
    count = lax.axis_size("blk")
    me = lax.axis_index("blk")
    nbits = count.bit_length() - 1
    order = [count // 2] + [1 << k for k in range(nbits - 1)]
    sparse = min(2, nbits)
    for bit in order[:sparse]:
        rows = jnp.concatenate([rows, _swap(rows, bit, count)])
        ids = jnp.concatenate([ids, _swap(ids, bit, count)])
        owner = ids // per
        ids = jnp.where((ids >= 0) & ((owner & bit) == (me & bit)), ids, -1)
    rest = order[sparse:]
    owner = ids // per
    slot = ids % per
    for k, bit in enumerate(rest):
        slot = slot + ((owner & bit) != 0).astype(jnp.int32) * (per << (len(rest) - 1 - k))
    hit = (slot[:, None] == jnp.arange(per << len(rest))[None, :]) & (ids >= 0)[:, None]
    dense = jnp.sum(jnp.where(hit[:, :, None, None], rows[:, None], 0.0), axis=0)
    for bit in rest:
        half = dense.shape[0] // 2
        upper = (me & bit) != 0
        keep = jnp.where(upper, dense[half:], dense[:half])
        send = jnp.where(upper, dense[:half], dense[half:])
        dense = keep + _swap(send, bit, count)
    return dense


def gather_tp(x):
    count = lax.axis_size("tp")
    me = lax.axis_index("tp")
    held = x[None]
    bit = count // 2
    while bit:
        got = lax.ppermute(held, "tp", [(i, i ^ bit) for i in range(count)])
        upper = (me & bit) != 0
        held = jnp.where(upper, jnp.stack([got, held], axis=1), jnp.stack([held, got], axis=1))
        held = held.reshape((-1,) + x.shape)
        bit //= 2
    return held.reshape((-1,) + x.shape[1:])


def reduce_scatter_tp(x, tie):
    count = lax.axis_size("tp")
    me = lax.axis_index("tp")
    nbits = count.bit_length() - 1
    held = x.reshape((2,) * nbits + (x.shape[0] // count,) + x.shape[1:])
    for k in range(nbits):
        bit = 1 << k
        axis = nbits - 1 - k
        low = lax.index_in_dim(held, 0, axis, keepdims=False)
        high = lax.index_in_dim(held, 1, axis, keepdims=False)
        upper = (me & bit) != 0
        keep = jnp.where(upper, high, low)
        send = jnp.where(upper, low, high)
        held = keep + lax.ppermute(send, "tp", [(i, i ^ bit) for i in range(count)])
        if k == 0:
            held, tie = lax.optimization_barrier((held, tie))
    return held, tie


def fetch_factors(rows, ids, per):
    count = lax.axis_size("blk")
    me = lax.axis_index("blk")
    nbits = count.bit_length() - 1
    order = [count // 2] + [1 << k for k in range(nbits - 1)]
    far, near = order[0], order[1]
    dense = order[2:][::-1]
    held = rows
    for bit in dense:
        got = _swap(held, bit, count)
        upper = (me & bit) != 0
        held = jnp.where(upper, jnp.concatenate([got, held]), jnp.concatenate([held, got]))
    group = far | near

    def lookup(want):
        owner = want // per
        k = want % per
        for i, bit in enumerate(dense):
            k = k + ((owner & bit) != 0).astype(jnp.int32) * (per << i)
        mine = (owner & group) == (me & group)
        found = jnp.take(held, k, axis=0)
        return mine, found, owner

    pair_ids = jnp.concatenate([ids, _swap(ids, far, count)])
    their_ids = _swap(pair_ids, near, count)
    mine, found, _ = lookup(their_ids)
    sent = jnp.where(mine[:, None, None], found, jnp.zeros_like(found))
    got = _swap(sent, near, count)
    mine, found, owner = lookup(pair_ids)
    side = (owner & far) == (me & far)
    cand = jnp.where(mine[:, None, None], found, got)
    half = ids.shape[0]
    got = _swap(cand[half:], far, count)
    return jnp.where(side[:half, None, None], cand[:half], got)


def on_device(tokens, weight, bank_a, bank_b, tile_map, grad_out):
    f32, bf16 = jnp.float32, jnp.bfloat16
    tile_ids = tile_map[:, 0]
    rows, feats = tokens.shape
    tiles = tile_ids.shape[0]
    tile_rows = rows // tiles
    rank_two = bank_a.shape[2]
    rank_one = rank_two // 2
    kv_width = bank_b.shape[2]
    tp_count = lax.axis_size("tp")
    tp_id = lax.axis_index("tp")
    kv_dev = kv_width // tp_count
    col0 = tp_id * kv_dev

    b_cols = lax.dynamic_slice_in_dim(bank_b, col0, kv_dev, 2)
    local = bank_a.shape[0]
    a_len = feats * rank_two // 128
    packed = jnp.concatenate([bank_a.reshape(local, -1, 128), b_cols.reshape(local, -1, 128)], axis=1)
    picked = fetch_factors(packed, tile_ids, local)
    grad_rows = gather_tp(grad_out)

    fac_a = picked[:, :a_len].reshape(tiles, feats, rank_two)
    fac_b = picked[:, a_len:].reshape(tiles, rank_two, kv_dev)

    tok_t = tokens.reshape(tiles, tile_rows, feats)
    act_part = jnp.einsum("tre,tek->trk", tok_t, fac_a, preferred_element_type=f32)

    g_t = grad_rows.reshape(tiles, tile_rows, 2 * kv_width)
    g_key = lax.dynamic_slice_in_dim(g_t, col0, kv_dev, 2)
    g_val = lax.dynamic_slice_in_dim(g_t, kv_width + col0, kv_dev, 2)
    grad_part = jnp.concatenate(
        [
            jnp.einsum("trc,tkc->trk", g_key, fac_b[:, :rank_one], preferred_element_type=f32),
            jnp.einsum("trc,tkc->trk", g_val, fac_b[:, rank_one:], preferred_element_type=f32),
        ],
        axis=2,
    )
    parts = jnp.stack([act_part, grad_part])
    flat_parts = parts.reshape(-1, 128)
    payload = jnp.concatenate([flat_parts, fac_b.astype(f32).reshape(-1, 128)])
    got = gather_axis(payload, "tp", 2)
    both = got[:, : flat_parts.shape[0]].sum(0).reshape(parts.shape)
    rank_act = both[0].astype(bf16)
    rank_grad = both[1].astype(bf16)
    full_b = got[:, flat_parts.shape[0] :].reshape(tp_count, tiles, rank_two, kv_dev)
    full_b = full_b.transpose(1, 2, 0, 3).reshape(tiles, rank_two, kv_width).astype(bf16)

    out_rows = rows // tp_count
    mine = max(1, out_rows // tile_rows)
    span = min(out_rows, tile_rows)
    first = tp_id * out_rows
    my_act = lax.dynamic_slice(rank_act, (first // tile_rows, first % tile_rows, 0), (mine, span, rank_two))
    my_b = lax.dynamic_slice(full_b, (first // tile_rows, 0, 0), (mine, rank_two, kv_width))
    lora = jnp.concatenate(
        [
            jnp.einsum("trk,tkc->trc", my_act[:, :, :rank_one], my_b[:, :rank_one], preferred_element_type=f32),
            jnp.einsum("trk,tkc->trc", my_act[:, :, rank_one:], my_b[:, rank_one:], preferred_element_type=f32),
        ],
        axis=2,
    ).reshape(out_rows, 2 * kv_width)

    backward = jnp.dot(grad_rows, weight.T, preferred_element_type=f32)
    adapter_back = jnp.einsum("tru,tyu->try", rank_grad, fac_a, preferred_element_type=f32)
    token_gradient = (backward + adapter_scale * adapter_back.reshape(rows, feats)).astype(bf16)

    down_grad = adapter_scale * jnp.einsum("tre,trk->tek", tok_t, rank_grad, preferred_element_type=f32)
    up_grad = adapter_scale * jnp.concatenate(
        [
            jnp.einsum("trk,trc->tkc", rank_act[:, :, :rank_one], g_key, preferred_element_type=f32),
            jnp.einsum("trk,trc->tkc", rank_act[:, :, rank_one:], g_val, preferred_element_type=f32),
        ],
        axis=1,
    )
    size_a = feats * rank_two
    flat = jnp.concatenate([down_grad.reshape(tiles, -1), up_grad.reshape(tiles, -1)], axis=1)
    base, fac_b = lax.optimization_barrier((jnp.dot(tokens, weight, preferred_element_type=f32), fac_b))

    summed = reduce_to_owner(flat.reshape(tiles, -1, 128), tile_ids, bank_a.shape[0]).reshape(bank_a.shape[0], -1)
    base_out, summed = reduce_scatter_tp(base, summed)
    key_value_output = (base_out + adapter_scale * lora).astype(bf16)
    grad_a = summed[:, :size_a].reshape(bank_a.shape[0], feats, rank_two)
    grad_b = summed[:, size_a:].reshape(bank_a.shape[0], rank_two, kv_dev)
    return (key_value_output, token_gradient, grad_a, grad_b)


def solution(mesh):
    in_specs = (
        P("blk", "tp"),
        P("tp", None),
        P("blk", "tp", None),
        P("blk", None, None),
        P("blk", None),
        P(("blk", "tp"), None),
    )
    out_specs = (P(("blk", "tp"), None), P("blk", "tp"), P("blk", "tp", None), P("blk", None, "tp"))
    return jax.shard_map(
        on_device, mesh=mesh, in_specs=in_specs, out_specs=out_specs, check_vma=False
    )
```

```python
import functools

import jax
import jax.numpy as jnp
from jax import lax
from jax.experimental import pallas as pl
from jax.experimental.pallas import tpu as pltpu
from jax.sharding import PartitionSpec as P

adapter_scale = 0.5
MESH = pl.DeviceIdType.MESH


def _peer(axis, me, other, k, n):
    peer = lax.rem(me + k, n)
    return (other, peer) if axis == "tp" else (peer, other)


def _gather_kernel(axis, n, x_ref, o_ref, slots, send_sem, recv_sem):
    me = lax.axis_index(axis)
    other = lax.axis_index("blk" if axis == "tp" else "tp")
    barrier = pltpu.get_barrier_semaphore()
    for k in range(1, n):
        pl.semaphore_signal(
            barrier, inc=1, device_id=_peer(axis, me, other, k, n), device_id_type=MESH
        )
    pl.semaphore_wait(barrier, n - 1)
    sends = []
    for k in range(1, n):
        copy = pltpu.make_async_remote_copy(
            src_ref=x_ref,
            dst_ref=slots.at[me],
            send_sem=send_sem.at[k],
            recv_sem=recv_sem.at[me],
            device_id=_peer(axis, me, other, k, n),
            device_id_type=MESH,
        )
        copy.start()
        sends.append(copy)
    slots[me] = x_ref[...]
    for k in range(1, n):
        src = lax.rem(me + n - k, n)
        pltpu.make_async_remote_copy(
            src_ref=x_ref,
            dst_ref=slots.at[src],
            send_sem=send_sem.at[k],
            recv_sem=recv_sem.at[src],
            device_id=_peer(axis, me, other, n - k, n),
            device_id_type=MESH,
        ).wait_recv()
    for copy in sends:
        copy.wait_send()
    o_ref[...] = slots[...]


def gather_axis(x, axis, cid):
    n = lax.axis_size(axis)
    return pl.pallas_call(
        functools.partial(_gather_kernel, axis, n),
        out_shape=jax.ShapeDtypeStruct((n,) + x.shape, x.dtype),
        in_specs=[pl.BlockSpec(memory_space=pltpu.VMEM)],
        out_specs=pl.BlockSpec(memory_space=pltpu.VMEM),
        scratch_shapes=[
            pltpu.VMEM((n,) + x.shape, x.dtype),
            pltpu.SemaphoreType.DMA((n,)),
            pltpu.SemaphoreType.DMA((n,)),
        ],
        compiler_params=pltpu.CompilerParams(collective_id=cid, has_side_effects=True),
    )(x)


def _swap(x, bit, count):
    return lax.ppermute(x, "blk", [(i, i ^ bit) for i in range(count)])


def reduce_to_owner(rows, ids, per):
    count = lax.axis_size("blk")
    me = lax.axis_index("blk")
    nbits = count.bit_length() - 1
    order = [count // 2] + [1 << k for k in range(nbits - 1)]
    sparse = min(2, nbits)
    for bit in order[:sparse]:
        rows = jnp.concatenate([rows, _swap(rows, bit, count)])
        ids = jnp.concatenate([ids, _swap(ids, bit, count)])
        owner = ids // per
        ids = jnp.where((ids >= 0) & ((owner & bit) == (me & bit)), ids, -1)
    rest = order[sparse:]
    owner = ids // per
    slot = ids % per
    for k, bit in enumerate(rest):
        slot = slot + ((owner & bit) != 0).astype(jnp.int32) * (per << (len(rest) - 1 - k))
    hit = (slot[:, None] == jnp.arange(per << len(rest))[None, :]) & (ids >= 0)[:, None]
    dense = jnp.sum(jnp.where(hit[:, :, None, None], rows[:, None], 0.0), axis=0)
    for bit in rest:
        half = dense.shape[0] // 2
        upper = (me & bit) != 0
        keep = jnp.where(upper, dense[half:], dense[:half])
        send = jnp.where(upper, dense[:half], dense[half:])
        dense = keep + _swap(send, bit, count)
    return dense


def gather_tp(x):
    count = lax.axis_size("tp")
    me = lax.axis_index("tp")
    held = x[None]
    bit = count // 2
    while bit:
        got = lax.ppermute(held, "tp", [(i, i ^ bit) for i in range(count)])
        upper = (me & bit) != 0
        held = jnp.where(upper, jnp.stack([got, held], axis=1), jnp.stack([held, got], axis=1))
        held = held.reshape((-1,) + x.shape)
        bit //= 2
    return held.reshape((-1,) + x.shape[1:])


def reduce_scatter_tp(x):
    count = lax.axis_size("tp")
    me = lax.axis_index("tp")
    nbits = count.bit_length() - 1
    held = x.reshape((2,) * nbits + (x.shape[0] // count,) + x.shape[1:])
    for k in range(nbits):
        bit = 1 << k
        axis = nbits - 1 - k
        low = lax.index_in_dim(held, 0, axis, keepdims=False)
        high = lax.index_in_dim(held, 1, axis, keepdims=False)
        upper = (me & bit) != 0
        keep = jnp.where(upper, high, low)
        send = jnp.where(upper, low, high)
        held = keep + lax.ppermute(send, "tp", [(i, i ^ bit) for i in range(count)])
    return held


def fetch_factors(rows, ids, per):
    count = lax.axis_size("blk")
    me = lax.axis_index("blk")
    nbits = count.bit_length() - 1
    order = [count // 2] + [1 << k for k in range(nbits - 1)]
    far, near = order[0], order[1]
    dense = order[2:][::-1]
    held = rows
    for bit in dense:
        got = _swap(held, bit, count)
        upper = (me & bit) != 0
        held = jnp.where(upper, jnp.concatenate([got, held]), jnp.concatenate([held, got]))
    group = far | near

    def lookup(want):
        owner = want // per
        k = want % per
        for i, bit in enumerate(dense):
            k = k + ((owner & bit) != 0).astype(jnp.int32) * (per << i)
        mine = (owner & group) == (me & group)
        found = jnp.take(held, k, axis=0)
        return mine, found, owner

    pair_ids = jnp.concatenate([ids, _swap(ids, far, count)])
    their_ids = _swap(pair_ids, near, count)
    mine, found, _ = lookup(their_ids)
    sent = jnp.where(mine[:, None, None], found, jnp.zeros_like(found))
    got = _swap(sent, near, count)
    mine, found, owner = lookup(pair_ids)
    side = (owner & far) == (me & far)
    cand = jnp.where(mine[:, None, None], found, got)
    half = ids.shape[0]
    got = _swap(cand[half:], far, count)
    return jnp.where(side[:half, None, None], cand[:half], got)


def on_device(tokens, weight, bank_a, bank_b, tile_map, grad_out):
    f32, bf16 = jnp.float32, jnp.bfloat16
    tile_ids = tile_map[:, 0]
    rows, feats = tokens.shape
    tiles = tile_ids.shape[0]
    tile_rows = rows // tiles
    rank_two = bank_a.shape[2]
    rank_one = rank_two // 2
    kv_width = bank_b.shape[2]
    tp_count = lax.axis_size("tp")
    tp_id = lax.axis_index("tp")
    kv_dev = kv_width // tp_count
    col0 = tp_id * kv_dev

    b_cols = lax.dynamic_slice_in_dim(bank_b, col0, kv_dev, 2)
    local = bank_a.shape[0]
    a_len = feats * rank_two // 128
    packed = jnp.concatenate([bank_a.reshape(local, -1, 128), b_cols.reshape(local, -1, 128)], axis=1)
    picked = fetch_factors(packed, tile_ids, local)
    grad_rows = gather_tp(grad_out)

    fac_a = picked[:, :a_len].reshape(tiles, feats, rank_two)
    fac_b = picked[:, a_len:].reshape(tiles, rank_two, kv_dev)

    tok_t = tokens.reshape(tiles, tile_rows, feats)
    act_part = jnp.einsum("tre,tek->trk", tok_t, fac_a, preferred_element_type=f32)

    g_t = grad_rows.reshape(tiles, tile_rows, 2 * kv_width)
    g_key = lax.dynamic_slice_in_dim(g_t, col0, kv_dev, 2)
    g_val = lax.dynamic_slice_in_dim(g_t, kv_width + col0, kv_dev, 2)
    grad_part = jnp.concatenate(
        [
            jnp.einsum("trc,tkc->trk", g_key, fac_b[:, :rank_one], preferred_element_type=f32),
            jnp.einsum("trc,tkc->trk", g_val, fac_b[:, rank_one:], preferred_element_type=f32),
        ],
        axis=2,
    )
    base, fac_b = lax.optimization_barrier((jnp.dot(tokens, weight, preferred_element_type=f32), fac_b))
    half = base.shape[1] // 2
    base_out = jnp.concatenate([reduce_scatter_tp(base[:, :half]), reduce_scatter_tp(base[:, half:])], axis=1)

    parts = jnp.stack([act_part, grad_part])
    flat_parts = parts.reshape(-1, 128)
    payload = jnp.concatenate([flat_parts, fac_b.astype(f32).reshape(-1, 128)])
    got = gather_axis(payload, "tp", 2)
    both = got[:, : flat_parts.shape[0]].sum(0).reshape(parts.shape)
    rank_act = both[0].astype(bf16)
    rank_grad = both[1].astype(bf16)
    full_b = got[:, flat_parts.shape[0] :].reshape(tp_count, tiles, rank_two, kv_dev)
    full_b = full_b.transpose(1, 2, 0, 3).reshape(tiles, rank_two, kv_width).astype(bf16)

    out_rows = rows // tp_count
    mine = max(1, out_rows // tile_rows)
    span = min(out_rows, tile_rows)
    first = tp_id * out_rows
    my_act = lax.dynamic_slice(rank_act, (first // tile_rows, first % tile_rows, 0), (mine, span, rank_two))
    my_b = lax.dynamic_slice(full_b, (first // tile_rows, 0, 0), (mine, rank_two, kv_width))
    lora = jnp.concatenate(
        [
            jnp.einsum("trk,tkc->trc", my_act[:, :, :rank_one], my_b[:, :rank_one], preferred_element_type=f32),
            jnp.einsum("trk,tkc->trc", my_act[:, :, rank_one:], my_b[:, rank_one:], preferred_element_type=f32),
        ],
        axis=2,
    ).reshape(out_rows, 2 * kv_width)
    key_value_output = (base_out + adapter_scale * lora).astype(bf16)

    backward = jnp.dot(grad_rows, weight.T, preferred_element_type=f32)
    adapter_back = jnp.einsum("tru,tyu->try", rank_grad, fac_a, preferred_element_type=f32)
    token_gradient = (backward + adapter_scale * adapter_back.reshape(rows, feats)).astype(bf16)

    down_grad = adapter_scale * jnp.einsum("tre,trk->tek", tok_t, rank_grad, preferred_element_type=f32)
    up_grad = adapter_scale * jnp.concatenate(
        [
            jnp.einsum("trk,trc->tkc", rank_act[:, :, :rank_one], g_key, preferred_element_type=f32),
            jnp.einsum("trk,trc->tkc", rank_act[:, :, rank_one:], g_val, preferred_element_type=f32),
        ],
        axis=1,
    )
    size_a = feats * rank_two
    flat = jnp.concatenate([down_grad.reshape(tiles, -1), up_grad.reshape(tiles, -1)], axis=1)
    summed = reduce_to_owner(flat.reshape(tiles, -1, 128), tile_ids, bank_a.shape[0]).reshape(bank_a.shape[0], -1)
    grad_a = summed[:, :size_a].reshape(bank_a.shape[0], feats, rank_two)
    grad_b = summed[:, size_a:].reshape(bank_a.shape[0], rank_two, kv_dev)
    return (key_value_output, token_gradient, grad_a, grad_b)


def solution(mesh):
    in_specs = (
        P("blk", "tp"),
        P("tp", None),
        P("blk", "tp", None),
        P("blk", None, None),
        P("blk", None),
        P(("blk", "tp"), None),
    )
    out_specs = (P(("blk", "tp"), None), P("blk", "tp"), P("blk", "tp", None), P("blk", None, "tp"))
    return jax.shard_map(
        on_device, mesh=mesh, in_specs=in_specs, out_specs=out_specs, check_vma=False
    )
```

```python
import functools

import jax
import jax.numpy as jnp
from jax import lax
from jax.experimental import pallas as pl
from jax.experimental.pallas import tpu as pltpu
from jax.sharding import PartitionSpec as P

adapter_scale = 0.5
MESH = pl.DeviceIdType.MESH


def _peer(axis, me, other, k, n):
    peer = lax.rem(me + k, n)
    return (other, peer) if axis == "tp" else (peer, other)


def _gather_kernel(axis, n, x_ref, o_ref, slots, send_sem, recv_sem):
    me = lax.axis_index(axis)
    other = lax.axis_index("blk" if axis == "tp" else "tp")
    barrier = pltpu.get_barrier_semaphore()
    for k in range(1, n):
        pl.semaphore_signal(
            barrier, inc=1, device_id=_peer(axis, me, other, k, n), device_id_type=MESH
        )
    pl.semaphore_wait(barrier, n - 1)
    sends = []
    for k in range(1, n):
        copy = pltpu.make_async_remote_copy(
            src_ref=x_ref,
            dst_ref=slots.at[me],
            send_sem=send_sem.at[k],
            recv_sem=recv_sem.at[me],
            device_id=_peer(axis, me, other, k, n),
            device_id_type=MESH,
        )
        copy.start()
        sends.append(copy)
    slots[me] = x_ref[...]
    for k in range(1, n):
        src = lax.rem(me + n - k, n)
        pltpu.make_async_remote_copy(
            src_ref=x_ref,
            dst_ref=slots.at[src],
            send_sem=send_sem.at[k],
            recv_sem=recv_sem.at[src],
            device_id=_peer(axis, me, other, n - k, n),
            device_id_type=MESH,
        ).wait_recv()
    for copy in sends:
        copy.wait_send()
    o_ref[...] = slots[...]


def gather_axis(x, axis, cid):
    n = lax.axis_size(axis)
    return pl.pallas_call(
        functools.partial(_gather_kernel, axis, n),
        out_shape=jax.ShapeDtypeStruct((n,) + x.shape, x.dtype),
        in_specs=[pl.BlockSpec(memory_space=pltpu.VMEM)],
        out_specs=pl.BlockSpec(memory_space=pltpu.VMEM),
        scratch_shapes=[
            pltpu.VMEM((n,) + x.shape, x.dtype),
            pltpu.SemaphoreType.DMA((n,)),
            pltpu.SemaphoreType.DMA((n,)),
        ],
        compiler_params=pltpu.CompilerParams(collective_id=cid, has_side_effects=True),
    )(x)


def _swap(x, bit, count):
    return lax.ppermute(x, "blk", [(i, i ^ bit) for i in range(count)])


def reduce_to_owner(rows, ids, per):
    count = lax.axis_size("blk")
    me = lax.axis_index("blk")
    nbits = count.bit_length() - 1
    order = [count // 2] + [1 << k for k in range(nbits - 1)]
    sparse = min(2, nbits)
    for bit in order[:sparse]:
        rows = jnp.concatenate([rows, _swap(rows, bit, count)])
        ids = jnp.concatenate([ids, _swap(ids, bit, count)])
        owner = ids // per
        ids = jnp.where((ids >= 0) & ((owner & bit) == (me & bit)), ids, -1)
    rest = order[sparse:]
    owner = ids // per
    slot = ids % per
    for k, bit in enumerate(rest):
        slot = slot + ((owner & bit) != 0).astype(jnp.int32) * (per << (len(rest) - 1 - k))
    hit = (slot[:, None] == jnp.arange(per << len(rest))[None, :]) & (ids >= 0)[:, None]
    dense = jnp.sum(jnp.where(hit[:, :, None, None], rows[:, None], 0.0), axis=0)
    for bit in rest:
        half = dense.shape[0] // 2
        upper = (me & bit) != 0
        keep = jnp.where(upper, dense[half:], dense[:half])
        send = jnp.where(upper, dense[:half], dense[half:])
        dense = keep + _swap(send, bit, count)
    return dense


def gather_tp(x):
    count = lax.axis_size("tp")
    me = lax.axis_index("tp")
    held = x[None]
    bit = count // 2
    while bit:
        got = lax.ppermute(held, "tp", [(i, i ^ bit) for i in range(count)])
        upper = (me & bit) != 0
        held = jnp.where(upper, jnp.stack([got, held], axis=1), jnp.stack([held, got], axis=1))
        held = held.reshape((-1,) + x.shape)
        bit //= 2
    return held.reshape((-1,) + x.shape[1:])


def reduce_scatter_tp(x):
    count = lax.axis_size("tp")
    me = lax.axis_index("tp")
    nbits = count.bit_length() - 1
    held = x.reshape((2,) * nbits + (x.shape[0] // count,) + x.shape[1:])
    left = [1 << (nbits - 1 - k) for k in range(nbits)]
    order = [1 << k for k in range(nbits)]
    order[:2] = order[1::-1]
    for bit in order:
        axis = left.index(bit)
        left.remove(bit)
        low = lax.index_in_dim(held, 0, axis, keepdims=False)
        high = lax.index_in_dim(held, 1, axis, keepdims=False)
        upper = (me & bit) != 0
        keep = jnp.where(upper, high, low)
        send = jnp.where(upper, low, high)
        held = keep + lax.ppermute(send, "tp", [(i, i ^ bit) for i in range(count)])
    return held


def fetch_factors(rows, ids, per):
    count = lax.axis_size("blk")
    me = lax.axis_index("blk")
    nbits = count.bit_length() - 1
    order = [count // 2] + [1 << k for k in range(nbits - 1)]
    far, near = order[0], order[1]
    dense = order[2:][::-1]
    held = rows
    for bit in dense:
        got = _swap(held, bit, count)
        upper = (me & bit) != 0
        held = jnp.where(upper, jnp.concatenate([got, held]), jnp.concatenate([held, got]))
    group = far | near

    def lookup(want):
        owner = want // per
        k = want % per
        for i, bit in enumerate(dense):
            k = k + ((owner & bit) != 0).astype(jnp.int32) * (per << i)
        mine = (owner & group) == (me & group)
        found = jnp.take(held, k, axis=0)
        return mine, found, owner

    pair_ids = jnp.concatenate([ids, _swap(ids, far, count)])
    their_ids = _swap(pair_ids, near, count)
    mine, found, _ = lookup(their_ids)
    sent = jnp.where(mine[:, None, None], found, jnp.zeros_like(found))
    got = _swap(sent, near, count)
    mine, found, owner = lookup(pair_ids)
    side = (owner & far) == (me & far)
    cand = jnp.where(mine[:, None, None], found, got)
    half = ids.shape[0]
    got = _swap(cand[half:], far, count)
    return jnp.where(side[:half, None, None], cand[:half], got)


def on_device(tokens, weight, bank_a, bank_b, tile_map, grad_out):
    f32, bf16 = jnp.float32, jnp.bfloat16
    tile_ids = tile_map[:, 0]
    rows, feats = tokens.shape
    tiles = tile_ids.shape[0]
    tile_rows = rows // tiles
    rank_two = bank_a.shape[2]
    rank_one = rank_two // 2
    kv_width = bank_b.shape[2]
    tp_count = lax.axis_size("tp")
    tp_id = lax.axis_index("tp")
    kv_dev = kv_width // tp_count
    col0 = tp_id * kv_dev

    b_cols = lax.dynamic_slice_in_dim(bank_b, col0, kv_dev, 2)
    local = bank_a.shape[0]
    a_len = feats * rank_two // 128
    packed = jnp.concatenate([bank_a.reshape(local, -1, 128), b_cols.reshape(local, -1, 128)], axis=1)
    picked = fetch_factors(packed, tile_ids, local)
    grad_rows = gather_tp(grad_out)

    fac_a = picked[:, :a_len].reshape(tiles, feats, rank_two)
    fac_b = picked[:, a_len:].reshape(tiles, rank_two, kv_dev)

    tok_t = tokens.reshape(tiles, tile_rows, feats)
    act_part = jnp.einsum("tre,tek->trk", tok_t, fac_a, preferred_element_type=f32)

    g_t = grad_rows.reshape(tiles, tile_rows, 2 * kv_width)
    g_key = lax.dynamic_slice_in_dim(g_t, col0, kv_dev, 2)
    g_val = lax.dynamic_slice_in_dim(g_t, kv_width + col0, kv_dev, 2)
    grad_part = jnp.concatenate(
        [
            jnp.einsum("trc,tkc->trk", g_key, fac_b[:, :rank_one], preferred_element_type=f32),
            jnp.einsum("trc,tkc->trk", g_val, fac_b[:, rank_one:], preferred_element_type=f32),
        ],
        axis=2,
    )
    base, fac_b = lax.optimization_barrier((jnp.dot(tokens, weight, preferred_element_type=f32), fac_b))
    base_out = reduce_scatter_tp(base)

    parts = jnp.stack([act_part, grad_part])
    flat_parts = parts.reshape(-1, 128)
    payload = jnp.concatenate([flat_parts, fac_b.astype(f32).reshape(-1, 128)])
    got = gather_axis(payload, "tp", 2)
    both = got[:, : flat_parts.shape[0]].sum(0).reshape(parts.shape)
    rank_act = both[0].astype(bf16)
    rank_grad = both[1].astype(bf16)
    full_b = got[:, flat_parts.shape[0] :].reshape(tp_count, tiles, rank_two, kv_dev)
    full_b = full_b.transpose(1, 2, 0, 3).reshape(tiles, rank_two, kv_width).astype(bf16)

    out_rows = rows // tp_count
    mine = max(1, out_rows // tile_rows)
    span = min(out_rows, tile_rows)
    first = tp_id * out_rows
    my_act = lax.dynamic_slice(rank_act, (first // tile_rows, first % tile_rows, 0), (mine, span, rank_two))
    my_b = lax.dynamic_slice(full_b, (first // tile_rows, 0, 0), (mine, rank_two, kv_width))
    lora = jnp.concatenate(
        [
            jnp.einsum("trk,tkc->trc", my_act[:, :, :rank_one], my_b[:, :rank_one], preferred_element_type=f32),
            jnp.einsum("trk,tkc->trc", my_act[:, :, rank_one:], my_b[:, rank_one:], preferred_element_type=f32),
        ],
        axis=2,
    ).reshape(out_rows, 2 * kv_width)
    key_value_output = (base_out + adapter_scale * lora).astype(bf16)

    backward = jnp.dot(grad_rows, weight.T, preferred_element_type=f32)
    adapter_back = jnp.einsum("tru,tyu->try", rank_grad, fac_a, preferred_element_type=f32)
    token_gradient = (backward + adapter_scale * adapter_back.reshape(rows, feats)).astype(bf16)

    down_grad = adapter_scale * jnp.einsum("tre,trk->tek", tok_t, rank_grad, preferred_element_type=f32)
    up_grad = adapter_scale * jnp.concatenate(
        [
            jnp.einsum("trk,trc->tkc", rank_act[:, :, :rank_one], g_key, preferred_element_type=f32),
            jnp.einsum("trk,trc->tkc", rank_act[:, :, rank_one:], g_val, preferred_element_type=f32),
        ],
        axis=1,
    )
    size_a = feats * rank_two
    flat = jnp.concatenate([down_grad.reshape(tiles, -1), up_grad.reshape(tiles, -1)], axis=1)
    summed = reduce_to_owner(flat.reshape(tiles, -1, 128), tile_ids, bank_a.shape[0]).reshape(bank_a.shape[0], -1)
    grad_a = summed[:, :size_a].reshape(bank_a.shape[0], feats, rank_two)
    grad_b = summed[:, size_a:].reshape(bank_a.shape[0], rank_two, kv_dev)
    return (key_value_output, token_gradient, grad_a, grad_b)


def solution(mesh):
    in_specs = (
        P("blk", "tp"),
        P("tp", None),
        P("blk", "tp", None),
        P("blk", None, None),
        P("blk", None),
        P(("blk", "tp"), None),
    )
    out_specs = (P(("blk", "tp"), None), P("blk", "tp"), P("blk", "tp", None), P("blk", None, "tp"))
    return jax.shard_map(
        on_device, mesh=mesh, in_specs=in_specs, out_specs=out_specs, check_vma=False
    )
```

```python
import functools

import jax
import jax.numpy as jnp
from jax import lax
from jax.experimental import pallas as pl
from jax.experimental.pallas import tpu as pltpu
from jax.sharding import PartitionSpec as P

adapter_scale = 0.5
MESH = pl.DeviceIdType.MESH


def _peer(axis, me, other, k, n):
    peer = lax.rem(me + k, n)
    return (other, peer) if axis == "tp" else (peer, other)


def _gather_kernel(axis, n, x_ref, o_ref, slots, send_sem, recv_sem):
    me = lax.axis_index(axis)
    other = lax.axis_index("blk" if axis == "tp" else "tp")
    barrier = pltpu.get_barrier_semaphore()
    for k in range(1, n):
        pl.semaphore_signal(
            barrier, inc=1, device_id=_peer(axis, me, other, k, n), device_id_type=MESH
        )
    pl.semaphore_wait(barrier, n - 1)
    sends = []
    for k in range(1, n):
        copy = pltpu.make_async_remote_copy(
            src_ref=x_ref,
            dst_ref=slots.at[me],
            send_sem=send_sem.at[k],
            recv_sem=recv_sem.at[me],
            device_id=_peer(axis, me, other, k, n),
            device_id_type=MESH,
        )
        copy.start()
        sends.append(copy)
    slots[me] = x_ref[...]
    for k in range(1, n):
        src = lax.rem(me + n - k, n)
        pltpu.make_async_remote_copy(
            src_ref=x_ref,
            dst_ref=slots.at[src],
            send_sem=send_sem.at[k],
            recv_sem=recv_sem.at[src],
            device_id=_peer(axis, me, other, n - k, n),
            device_id_type=MESH,
        ).wait_recv()
    for copy in sends:
        copy.wait_send()
    o_ref[...] = slots[...]


def gather_axis(x, axis, cid):
    n = lax.axis_size(axis)
    return pl.pallas_call(
        functools.partial(_gather_kernel, axis, n),
        out_shape=jax.ShapeDtypeStruct((n,) + x.shape, x.dtype),
        in_specs=[pl.BlockSpec(memory_space=pltpu.VMEM)],
        out_specs=pl.BlockSpec(memory_space=pltpu.VMEM),
        scratch_shapes=[
            pltpu.VMEM((n,) + x.shape, x.dtype),
            pltpu.SemaphoreType.DMA((n,)),
            pltpu.SemaphoreType.DMA((n,)),
        ],
        compiler_params=pltpu.CompilerParams(collective_id=cid, has_side_effects=True),
    )(x)


def _swap(x, bit, count):
    return lax.ppermute(x, "blk", [(i, i ^ bit) for i in range(count)])


def reduce_to_owner(rows, ids, per):
    count = lax.axis_size("blk")
    me = lax.axis_index("blk")
    nbits = count.bit_length() - 1
    order = [count // 2] + [1 << k for k in range(nbits - 1)]
    sparse = min(2, nbits)
    for bit in order[:sparse]:
        rows = jnp.concatenate([rows, _swap(rows, bit, count)])
        ids = jnp.concatenate([ids, _swap(ids, bit, count)])
        owner = ids // per
        ids = jnp.where((ids >= 0) & ((owner & bit) == (me & bit)), ids, -1)
    rest = order[sparse:]
    owner = ids // per
    slot = ids % per
    for k, bit in enumerate(rest):
        slot = slot + ((owner & bit) != 0).astype(jnp.int32) * (per << (len(rest) - 1 - k))
    hit = (slot[:, None] == jnp.arange(per << len(rest))[None, :]) & (ids >= 0)[:, None]
    dense = jnp.sum(jnp.where(hit[:, :, None, None], rows[:, None], 0.0), axis=0)
    for bit in rest:
        half = dense.shape[0] // 2
        upper = (me & bit) != 0
        keep = jnp.where(upper, dense[half:], dense[:half])
        send = jnp.where(upper, dense[:half], dense[half:])
        dense = keep + _swap(send, bit, count)
    return dense


def gather_tp(x):
    count = lax.axis_size("tp")
    me = lax.axis_index("tp")
    held = x[None]
    bit = 1
    while bit < count:
        got = lax.ppermute(held, "tp", [(i, i ^ bit) for i in range(count)])
        upper = (me & bit) != 0
        held = jnp.where(upper, jnp.concatenate([got, held]), jnp.concatenate([held, got]))
        bit *= 2
    return held.reshape((-1,) + x.shape[1:])


def reduce_scatter_tp(x):
    count = lax.axis_size("tp")
    me = lax.axis_index("tp")
    nbits = count.bit_length() - 1
    held = x.reshape((2,) * nbits + (x.shape[0] // count,) + x.shape[1:])
    left = [1 << (nbits - 1 - k) for k in range(nbits)]
    order = [1 << k for k in range(nbits)]
    order[:2] = order[1::-1]
    for bit in order:
        axis = left.index(bit)
        left.remove(bit)
        low = lax.index_in_dim(held, 0, axis, keepdims=False)
        high = lax.index_in_dim(held, 1, axis, keepdims=False)
        upper = (me & bit) != 0
        keep = jnp.where(upper, high, low)
        send = jnp.where(upper, low, high)
        held = keep + lax.ppermute(send, "tp", [(i, i ^ bit) for i in range(count)])
    return held


def fetch_factors(rows, ids, per):
    count = lax.axis_size("blk")
    me = lax.axis_index("blk")
    nbits = count.bit_length() - 1
    order = [count // 2] + [1 << k for k in range(nbits - 1)]
    far, near = order[0], order[1]
    dense = order[2:][::-1]
    held = rows
    for bit in dense:
        got = _swap(held, bit, count)
        upper = (me & bit) != 0
        held = jnp.where(upper, jnp.concatenate([got, held]), jnp.concatenate([held, got]))
    group = far | near

    def lookup(want):
        owner = want // per
        k = want % per
        for i, bit in enumerate(dense):
            k = k + ((owner & bit) != 0).astype(jnp.int32) * (per << i)
        mine = (owner & group) == (me & group)
        found = jnp.take(held, k, axis=0)
        return mine, found, owner

    pair_ids = jnp.concatenate([ids, _swap(ids, far, count)])
    their_ids = _swap(pair_ids, near, count)
    mine, found, _ = lookup(their_ids)
    sent = jnp.where(mine[:, None, None], found, jnp.zeros_like(found))
    got = _swap(sent, near, count)
    mine, found, owner = lookup(pair_ids)
    side = (owner & far) == (me & far)
    cand = jnp.where(mine[:, None, None], found, got)
    half = ids.shape[0]
    got = _swap(cand[half:], far, count)
    return jnp.where(side[:half, None, None], cand[:half], got)


def on_device(tokens, weight, bank_a, bank_b, tile_map, grad_out):
    f32, bf16 = jnp.float32, jnp.bfloat16
    tile_ids = tile_map[:, 0]
    rows, feats = tokens.shape
    tiles = tile_ids.shape[0]
    tile_rows = rows // tiles
    rank_two = bank_a.shape[2]
    rank_one = rank_two // 2
    kv_width = bank_b.shape[2]
    tp_count = lax.axis_size("tp")
    tp_id = lax.axis_index("tp")
    kv_dev = kv_width // tp_count
    col0 = tp_id * kv_dev

    b_cols = lax.dynamic_slice_in_dim(bank_b, col0, kv_dev, 2)
    local = bank_a.shape[0]
    a_len = feats * rank_two // 128
    packed = jnp.concatenate([bank_a.reshape(local, -1, 128), b_cols.reshape(local, -1, 128)], axis=1)
    picked = fetch_factors(packed, tile_ids, local)
    grad_rows = gather_tp(grad_out)

    fac_a = picked[:, :a_len].reshape(tiles, feats, rank_two)
    fac_b = picked[:, a_len:].reshape(tiles, rank_two, kv_dev)

    tok_t = tokens.reshape(tiles, tile_rows, feats)
    act_part = jnp.einsum("tre,tek->trk", tok_t, fac_a, preferred_element_type=f32)

    g_t = grad_rows.reshape(tiles, tile_rows, 2 * kv_width)
    g_key = lax.dynamic_slice_in_dim(g_t, col0, kv_dev, 2)
    g_val = lax.dynamic_slice_in_dim(g_t, kv_width + col0, kv_dev, 2)
    grad_part = jnp.concatenate(
        [
            jnp.einsum("trc,tkc->trk", g_key, fac_b[:, :rank_one], preferred_element_type=f32),
            jnp.einsum("trc,tkc->trk", g_val, fac_b[:, rank_one:], preferred_element_type=f32),
        ],
        axis=2,
    )
    base, fac_b = lax.optimization_barrier((jnp.dot(tokens, weight, preferred_element_type=f32), fac_b))
    base_out = reduce_scatter_tp(base)

    parts = jnp.stack([act_part, grad_part])
    flat_parts = parts.reshape(-1, 128)
    payload = jnp.concatenate([flat_parts, fac_b.astype(f32).reshape(-1, 128)])
    got = gather_axis(payload, "tp", 2)
    both = got[:, : flat_parts.shape[0]].sum(0).reshape(parts.shape)
    rank_act = both[0].astype(bf16)
    rank_grad = both[1].astype(bf16)
    full_b = got[:, flat_parts.shape[0] :].reshape(tp_count, tiles, rank_two, kv_dev)
    full_b = full_b.transpose(1, 2, 0, 3).reshape(tiles, rank_two, kv_width).astype(bf16)

    out_rows = rows // tp_count
    mine = max(1, out_rows // tile_rows)
    span = min(out_rows, tile_rows)
    first = tp_id * out_rows
    my_act = lax.dynamic_slice(rank_act, (first // tile_rows, first % tile_rows, 0), (mine, span, rank_two))
    my_b = lax.dynamic_slice(full_b, (first // tile_rows, 0, 0), (mine, rank_two, kv_width))
    lora = jnp.concatenate(
        [
            jnp.einsum("trk,tkc->trc", my_act[:, :, :rank_one], my_b[:, :rank_one], preferred_element_type=f32),
            jnp.einsum("trk,tkc->trc", my_act[:, :, rank_one:], my_b[:, rank_one:], preferred_element_type=f32),
        ],
        axis=2,
    ).reshape(out_rows, 2 * kv_width)
    key_value_output = (base_out + adapter_scale * lora).astype(bf16)

    backward = jnp.dot(grad_rows, weight.T, preferred_element_type=f32)
    adapter_back = jnp.einsum("tru,tyu->try", rank_grad, fac_a, preferred_element_type=f32)
    token_gradient = (backward + adapter_scale * adapter_back.reshape(rows, feats)).astype(bf16)

    down_grad = adapter_scale * jnp.einsum("tre,trk->tek", tok_t, rank_grad, preferred_element_type=f32)
    up_grad = adapter_scale * jnp.concatenate(
        [
            jnp.einsum("trk,trc->tkc", rank_act[:, :, :rank_one], g_key, preferred_element_type=f32),
            jnp.einsum("trk,trc->tkc", rank_act[:, :, rank_one:], g_val, preferred_element_type=f32),
        ],
        axis=1,
    )
    size_a = feats * rank_two
    flat = jnp.concatenate([down_grad.reshape(tiles, -1), up_grad.reshape(tiles, -1)], axis=1)
    summed = reduce_to_owner(flat.reshape(tiles, -1, 128), tile_ids, bank_a.shape[0]).reshape(bank_a.shape[0], -1)
    grad_a = summed[:, :size_a].reshape(bank_a.shape[0], feats, rank_two)
    grad_b = summed[:, size_a:].reshape(bank_a.shape[0], rank_two, kv_dev)
    return (key_value_output, token_gradient, grad_a, grad_b)


def solution(mesh):
    in_specs = (
        P("blk", "tp"),
        P("tp", None),
        P("blk", "tp", None),
        P("blk", None, None),
        P("blk", None),
        P(("blk", "tp"), None),
    )
    out_specs = (P(("blk", "tp"), None), P("blk", "tp"), P("blk", "tp", None), P("blk", None, "tp"))
    return jax.shard_map(
        on_device, mesh=mesh, in_specs=in_specs, out_specs=out_specs, check_vma=False
    )
```
